256 devices in a mesh: gx: 32 (over z_lo, x, core), gy: 8 (over y, z_hi).
Axes of the slice: x: 4, y: 4, z: 8 (z_hi: 2, z_lo: 4; z = z_hi * 4 + z_lo), core: 2. Of those that a mesh axis runs over, the one named last changes fastest.
Arguments:
- source: float32 [2, 8, 4096, 2048], P(None, None, 'gx', 'gy'), may hold values from -6 to 6
- transmissibility: bfloat16 [4, 8, 4096, 2048], P(None, None, 'gx', 'gy'), may hold values from 0.099609375 to 1
- diagonal: float32 [2, 8, 4096, 2048], P(None, None, 'gx', 'gy'), may hold values from 4.6 to 7
- upwind_flags: int32 [8, 4096, 2048], P(None, 'gx', 'gy'), may hold values from 0 to 15
- panel_coef: bfloat16 [32, 8, 16, 32, 128], P('gx', 'gy'), may hold values from -0.5 to 0.5
- perf_cell: int32 [32, 8, 16, 128], P('gx', 'gy'), may hold values from 0 to 262143
- panel_well: int32 [32, 8, 16], P('gx', 'gy'), may hold values from 0 to 31
- seg_count: int32 [32, 32], P('gx'), may hold values from 1 to 32, as said below
- well_inverse: float32 [32, 32, 32, 32], P('gx'), may hold values from -1 to 1
Outputs:
- adjoint: float32 [2, 8, 4096, 2048], P(None, None, 'gx', 'gy')
The draws below stay inside these ranges and needn't reach their ends.
Inputs may be any that keep to these rules, and one draw needn't show every extreme that they name: `seg_count`: some well of every group has 32 segments and some has one.
All inputs are finite; a program needn't handle non-finite values.
Results may differ from the reference program's by a relative error of at most 0.0003.
Values may be sent and summed in bfloat16 or wider, within the bound.
A program may use at most 64 MiB of HBM per device.

```python
import math
import jax
import jax.numpy as jnp
import numpy as np
from jax import lax

NL = 8
CX = 128
CY = 256
PANELS = 16
PERF = 128
NSEG = 32
WELLS = 32
ITERS = 3
CELLS_DEV = 262144
NX = 4096
NY = 2048
N_GX = 32
N_GY = 8


def draw_seg_count(key, part):
    values = jax.random.randint(key, (N_GX, WELLS), 1, NSEG + 1)
    first = jax.random.randint(jax.random.fold_in(key, 11), (N_GX,), 0, WELLS)
    offset = jax.random.randint(jax.random.fold_in(key, 12), (N_GX,), 1, WELLS)
    second = (first + offset) % WELLS
    column = jnp.arange(WELLS, dtype=jnp.int32)[None, :]
    values = jnp.where(column == first[:, None], NSEG, values)
    values = jnp.where(column == second[:, None], 1, values)
    return values.astype(jnp.int32)


def with_ends(array, stream_key, least, high):
    place = [jax.random.randint(jax.random.fold_in(stream_key, axis), (), 0, length) for axis, length in enumerate(array.shape)]
    main_axis = array.shape.index(max(array.shape))
    next_to = place[:main_axis] + [(place[main_axis] + 1) % array.shape[main_axis]] + place[main_axis + 1:]
    return array.at[tuple(place)].set(least).at[tuple(next_to)].set(high)


def levels(stream_key, dims, pieces, low, high):
    def one(axis_at, blocks):
        steps = jax.random.uniform(jax.random.fold_in(jax.random.fold_in(stream_key, 6), axis_at), (blocks,), jnp.float32, low / len(pieces), high / len(pieces))
        return jnp.repeat(jnp.exp(steps), dims[axis_at] // blocks).reshape((-1,) + (1,) * (len(dims) - axis_at - 1))

    level = one(*pieces[0])
    for cut in pieces[1:]:
        level = level * one(*cut)
    return level


def rank_table(count, lean):
    loads = [(1 << 20) // math.isqrt(grade ** lean) + 1 for grade in range(1, count + 1)]
    spread = 1 + sum(loads) // (1 << 30)
    return np.cumsum(np.array([max(1, weight // spread) for weight in loads]))


def skewed_ids(stream_key, extent, number_of, skew):
    grid = rank_table(number_of, skew)
    pick = jax.random.randint(jax.random.fold_in(stream_key, 1), extent, 0, int(grid[number_of - 1]))
    standing = jnp.searchsorted(jnp.asarray(grid, jnp.int32), pick, side="right")
    return jax.random.permutation(jax.random.fold_in(stream_key, 2), number_of)[standing].astype(jnp.int32)


def scatter_about(stream_key, dims, width, most, pieces=(), kind=jnp.bfloat16):
    factor_of = levels(stream_key, dims, pieces, -0.22, 0.18) if pieces else 1.0
    drawn = jax.random.normal(stream_key, dims, jnp.float32) * width * factor_of
    return jnp.minimum(jnp.maximum(drawn, -most), most).astype(kind)


def setup_inputs(seed: int = 0) -> dict:
    key_list = jax.random.split(jax.random.key(seed), 10)
    return {
        "source": scatter_about(key_list[0], (2, NL, NX, NY), 1.0, 6.0, ((2, 32), (3, 8)), jnp.float32),
        "transmissibility": jnp.clip(jnp.exp(math.log(1.0) - 2.306499 * jax.random.uniform(key_list[1], (4, NL, NX, NY), jnp.float32) ** levels(key_list[1], (4, NL, NX, NY), ((2, 32), (3, 8)), -0.2, 0.2)), 0.099609375, 1.0).astype(jnp.bfloat16),
        "diagonal": jnp.clip(4.6 + 2.4 * jax.random.uniform(key_list[2], (2, NL, NX, NY), jnp.float32) ** levels(key_list[2], (2, NL, NX, NY), ((2, 32), (3, 8)), -0.2, 0.2), 4.6, 7.0),
        "upwind_flags": with_ends(jax.random.randint(key_list[3], (NL, NX, NY), 0, 16), jax.random.fold_in(key_list[3], 1), 0, 15).astype(jnp.int32),
        "panel_coef": scatter_about(key_list[4], (N_GX, N_GY, PANELS, NSEG, PERF), PERF ** -0.5, 0.5, ((0, 32), (1, 8))),
        "perf_cell": with_ends(jax.random.randint(key_list[5], (N_GX, N_GY, PANELS, PERF), 0, CELLS_DEV), jax.random.fold_in(key_list[5], 1), 0, CELLS_DEV - 1).astype(jnp.int32),
        "panel_well": with_ends(skewed_ids(key_list[6], (N_GX, N_GY, PANELS), WELLS, 2), jax.random.fold_in(key_list[6], 3), 0, WELLS - 1).astype(jnp.int32),
        "seg_count": draw_seg_count(jax.random.fold_in(key_list[9], 71), 0),
        "well_inverse": scatter_about(key_list[8], (N_GX, WELLS, NSEG, NSEG), NSEG ** -0.5, 1.0, ((0, 32),), jnp.float32),
    }


def neighbours(field):
    padded = jnp.pad(field, ((0, 0), (0, 0), (1, 1), (1, 1)))
    return [padded[:, :, :-2, 1:-1], padded[:, :, 2:, 1:-1], padded[:, :, 1:-1, :-2], padded[:, :, 1:-1, 2:]]


def jacobi(state, source, trans, diagonal, flags):
    near = neighbours(state)
    pres = state[0]
    pres_sum = source[0]
    sat_sum = source[1]
    for k in range(4):
        upwind = jnp.bitwise_and(jnp.right_shift(flags, k), 1).astype(jnp.float32)
        weight = trans[k]
        pres_sum = pres_sum + weight * near[k][0]
        sat_sum = sat_sum + weight * upwind * near[k][1] + 0.3 * weight * upwind * (near[k][0] - pres)
    return pres_sum / diagonal[0], sat_sum / diagonal[1]


def reference(source, transmissibility, diagonal, upwind_flags, panel_coef, perf_cell, panel_well, seg_count, well_inverse):
    trans = transmissibility.astype(jnp.float32)
    coef = panel_coef.astype(jnp.float32)
    high = lax.Precision.HIGHEST
    seg_mask = (jnp.arange(NSEG, dtype=jnp.int32)[None, None, :] < seg_count[:, :, None]).astype(jnp.float32)
    onehot = (panel_well[..., None] == jnp.arange(WELLS, dtype=jnp.int32)).astype(jnp.float32)
    perf_flat = perf_cell.reshape(N_GX, N_GY, PANELS * PERF)
    rows_a = jnp.arange(N_GX, dtype=jnp.int32)[:, None, None]
    rows_b = jnp.arange(N_GY, dtype=jnp.int32)[None, :, None]
    state = source
    for step in range(ITERS):
        pres, sat = jacobi(state, source, trans, diagonal, upwind_flags)
        blocks = pres.reshape(NL, N_GX, CX, N_GY, CY).transpose(1, 3, 0, 2, 4).reshape(N_GX, N_GY, CELLS_DEV)
        samples = jnp.take_along_axis(blocks, perf_flat, axis=2).reshape(N_GX, N_GY, PANELS, PERF)
        partial_sums = jnp.einsum("abqsr,abqr->abqs", coef, samples, precision=high)
        residual = jnp.einsum("abqw,abqs->aws", onehot, partial_sums, precision=high) * seg_mask
        solved = jnp.einsum("awst,awt->aws", well_inverse, residual, precision=high) * seg_mask
        per_block = jnp.einsum("abqw,aws->abqs", onehot, solved, precision=high)
        correction = jnp.einsum("abqsr,abqs->abqr", coef, per_block, precision=high)
        blocks = blocks.at[rows_a, rows_b, perf_flat].add(-correction.reshape(N_GX, N_GY, PANELS * PERF))
        pres = blocks.reshape(N_GX, N_GY, NL, CX, CY).transpose(2, 0, 3, 1, 4).reshape(NL, NX, NY)
        state = jnp.stack([pres, sat])
    return state
```

```python
import functools

import jax
import jax.numpy as jnp
from jax import lax
from jax.experimental import pallas as pl
from jax.experimental.pallas import tpu as pltpu
from jax.sharding import PartitionSpec as P

ITERS = 3
MESH = pl.DeviceIdType.MESH
F32 = jnp.float32
BF16 = jnp.bfloat16
W, E, S, N = 0, 1, 2, 3
CH = 16


def lane_pick(x, idx):
    return jnp.take_along_axis(x, idx, axis=1, mode="promise_in_bounds")


def kernel(
    n_gx,
    n_gy,
    row_idx,
    well_s,
    count_s,
    src,
    trans,
    diag,
    flags,
    coef,
    cells,
    inv,
    out,
    pbuf,
    sbuf,
    tu,
    rdiag,
    ut,
    cvt,
    res,
    lanes_r,
    kmat,
    samp,
    corr,
    srow,
    rrow,
    scol,
    rcol,
    wsend,
    wall,
    agsend,
    ag,
    ss_row,
    rs_row,
    ss_col,
    rs_col,
    ss_w,
    rs_w,
    ss_ag,
    rs_ag,
):
    gx = lax.axis_index("gx")
    gy = lax.axis_index("gy")
    there = (gx > 0, gx < n_gx - 1, gy > 0, gy < n_gy - 1)
    peer_id = ({"gx": gx - 1}, {"gx": gx + 1}, {"gy": gy - 1}, {"gy": gy + 1})
    layers = src.shape[1]
    blocks = coef.shape[0]
    segs = coef.shape[1]
    groups = segs // 8

    sub8 = lax.broadcasted_iota(jnp.int32, (8, 128), 0)
    lane8 = lax.broadcasted_iota(jnp.int32, (8, 128), 1)
    subc = lax.broadcasted_iota(jnp.int32, (CH, 128), 0)
    lanec = lax.broadcasted_iota(jnp.int32, (CH, 128), 1)

    barrier = pltpu.get_barrier_semaphore()
    for d in range(1, n_gy):
        pl.semaphore_signal(
            barrier, inc=1, device_id={"gy": lax.rem(gy + d, n_gy)}, device_id_type=MESH
        )
    for k in (W, E):

        @pl.when(there[k])
        def _():
            pl.semaphore_signal(barrier, inc=1, device_id=peer_id[k], device_id_type=MESH)

    beside = jnp.where(there[W], 1, 0) + jnp.where(there[E], 1, 0)
    pl.semaphore_wait(barrier, n_gy - 1 + beside)

    def halo_copy(it, f, k, dst_side):
        if k in (W, E):
            return pltpu.make_async_remote_copy(
                src_ref=srow.at[it, f, k],
                dst_ref=rrow.at[it, f, dst_side],
                send_sem=ss_row.at[it, f, k],
                recv_sem=rs_row.at[it, f, dst_side],
                device_id=peer_id[k],
                device_id_type=MESH,
            )
        return pltpu.make_async_remote_copy(
            src_ref=scol.at[it, f, k - 2],
            dst_ref=rcol.at[it, f, dst_side - 2],
            send_sem=ss_col.at[it, f, k - 2],
            recv_sem=rs_col.at[it, f, dst_side - 2],
            device_id=peer_id[k],
            device_id_type=MESH,
        )

    def halo_send(buf, par, it, f):
        srow[it, f, W] = buf[par, :, 0, :]
        srow[it, f, E] = buf[par, :, 127, :]
        for k in (W, E):

            @pl.when(there[k])
            def _():
                halo_copy(it, f, k, 1 - k).start()

        @pl.loop(0, layers)
        def _(l):
            for side, half, lane in ((0, 0, 0), (1, 1, 127)):
                acc = jnp.zeros((8, 128), F32)
                for g in range(16):
                    v = buf[par, 2 * l + half, 8 * g : 8 * g + 8, :]
                    b = jnp.broadcast_to(v[:, lane : lane + 1], (8, 128))
                    acc = jnp.where(lane8 == sub8 + 8 * g, b, acc)
                scol[it, f, side, pl.ds(l, 1), :] = jnp.sum(acc, axis=0, keepdims=True)

        for k in (S, N):

            @pl.when(there[k])
            def _():
                halo_copy(it, f, k, 5 - k).start()

    def halo_wait(it, f):
        for k in (W, E, S, N):

            @pl.when(there[k])
            def _():
                halo_copy(it, f, k, k).wait_recv()

    def peer_copy(src_ref, dst_ref, send_sem, recv_sem, d):
        return pltpu.make_async_remote_copy(
            src_ref=src_ref,
            dst_ref=dst_ref,
            send_sem=send_sem,
            recv_sem=recv_sem,
            device_id={"gy": lax.rem(gy + d, n_gy)},
            device_id_type=MESH,
        )

    wrow = jnp.zeros((8, 128), jnp.int32)
    for q in range(blocks):
        wrow = jnp.where(lax.rem(lane8, blocks) == q, well_s[q], wrow)
    wsend[...] = wrow
    wall[gy] = wrow
    for d in range(1, n_gy):
        peer_copy(wsend, wall.at[gy], ss_w.at[d - 1], rs_w.at[gy], d).start()

    for l in range(layers):
        for h in range(2):
            pbuf[0, 2 * l + h] = src[0, l, :, h * 128 : h * 128 + 128]
            sbuf[0, 2 * l + h] = src[1, l, :, h * 128 : h * 128 + 128]
    halo_send(pbuf, 0, 0, 0)
    halo_send(sbuf, 0, 0, 1)
    for k in (W, E):

        @pl.when(jnp.logical_not(there[k]))
        def _():
            for it in range(ITERS):
                for f in range(2):
                    rrow[it, f, k] = jnp.zeros((16, 128), F32)

    for k in (S, N):

        @pl.when(jnp.logical_not(there[k]))
        def _():
            for it in range(ITERS):
                for f in range(2):
                    rcol[it, f, k - 2] = jnp.zeros((8, 128), F32)

    @pl.loop(0, layers)
    def _(l):
        for c in range(128 // CH):
            rows = slice(c * CH, c * CH + CH)
            for f in range(2):
                rdiag[f, l, rows, :] = 1.0 / diag[f, l, rows, :]
            fl = flags[l, rows, :]
            for k in range(4):
                bit = jnp.bitwise_and(jnp.right_shift(fl, k), 1)
                t = trans[k, l, rows, :].astype(F32)
                tu[k, l, rows, :] = jnp.where(bit == 1, t, 0.0).astype(BF16)

    @pl.loop(0, blocks)
    def _(q):
        row = cells[pl.ds(q, 1), :]
        lane = jnp.broadcast_to(jnp.bitwise_and(row, 127), (128, 128))
        lanes_r[pl.ds(pl.multiple_of(q * 128, 128), 128), :] = lane.T
        w = well_s[q]
        count = count_s[w]
        i0 = lax.broadcasted_iota(jnp.int32, (segs, segs), 0)
        i1 = lax.broadcasted_iota(jnp.int32, (segs, segs), 1)
        m = jnp.where(jnp.logical_and(i0 < count, i1 < count), inv[w], 0.0)
        kmat[q] = lax.dot_general(
            m,
            coef[q].astype(F32),
            (((0,), (0,)), ((), ())),
            precision=lax.Precision.HIGHEST,
            preferred_element_type=F32,
        )

    @pl.loop(0, ut.shape[0] // 32)
    def _(i):
        i32 = lax.broadcasted_iota(jnp.int32, (32, 128), 0) + i * 32
        for q in range(blocks):
            a = jnp.right_shift(cells[q : q + 1, :], 8)
            hot = jnp.where(i32 == a, 1.0, 0.0).astype(BF16)
            ut[pl.ds(pl.multiple_of(i * 32, 32), 32), q * 128 : q * 128 + 128] = hot

    for d in range(1, n_gy):
        peer = lax.rem(gy + d, n_gy)
        peer_copy(wsend, wall.at[peer], ss_w.at[d - 1], rs_w.at[peer], d).wait_recv()

    def shifted(ref, par, l, c):
        r0 = c * CH
        mid, west, east = [], [], []
        for h in range(2):
            x = ref[par, 2 * l + h, r0 : r0 + CH, :]
            mid.append(x)
            if c == 0:
                west.append(jnp.where(subc == 0, 0.0, pltpu.roll(x, 1, 0)))
            else:
                west.append(ref[par, 2 * l + h, r0 - 1 : r0 + CH - 1, :])
            if c == 128 // CH - 1:
                east.append(jnp.where(subc == CH - 1, 0.0, pltpu.roll(x, CH - 1, 0)))
            else:
                east.append(ref[par, 2 * l + h, r0 + 1 : r0 + CH + 1, :])
        up = [pltpu.roll(x, 1, 1) for x in mid]
        down = [pltpu.roll(x, 127, 1) for x in mid]
        south = [jnp.where(lanec == 0, 0.0, up[0]), jnp.where(lanec == 0, up[0], up[1])]
        north = [
            jnp.where(lanec == 127, down[1], down[0]),
            jnp.where(lanec == 127, 0.0, down[1]),
        ]
        return mid, (west, east, south, north)

    def p_inner(par, nxt):
        @pl.loop(0, layers)
        def _(l):
            for c in range(128 // CH):
                rows = slice(c * CH, c * CH + CH)
                _, near = shifted(pbuf, par, l, c)
                for h in range(2):
                    cols = slice(h * 128, h * 128 + 128)
                    acc = src[0, l, rows, cols]
                    for k in range(4):
                        acc = acc + trans[k, l, rows, cols].astype(F32) * near[k][h]
                    pbuf[nxt, 2 * l + h, rows, :] = acc * rdiag[0, l, rows, cols]

    def s_inner(par, nxt):
        @pl.loop(0, layers)
        def _(l):
            for c in range(128 // CH):
                rows = slice(c * CH, c * CH + CH)
                midp, nearp = shifted(pbuf, par, l, c)
                _, nears = shifted(sbuf, par, l, c)
                for h in range(2):
                    cols = slice(h * 128, h * 128 + 128)
                    acc = src[1, l, rows, cols]
                    p3 = 0.3 * midp[h]
                    for k in range(4):
                        g = (nears[k][h] + 0.3 * nearp[k][h]) - p3
                        acc = acc + tu[k, l, rows, cols].astype(F32) * g
                    sbuf[nxt, 2 * l + h, rows, :] = acc * rdiag[1, l, rows, cols]

    def add_halo(it, f, tt, dst, nxt):
        def row(k, l, h):
            x = rrow[it, f, k, pl.ds(2 * l + h, 1), :]
            if f == 1:
                x = x + 0.3 * rrow[it, 0, k, pl.ds(2 * l + h, 1), :]
            return x

        def col(k, l):
            x = rcol[it, f, k - 2, pl.ds(l, 1), :]
            if f == 1:
                x = x + 0.3 * rcol[it, 0, k - 2, pl.ds(l, 1), :]
            return jnp.broadcast_to(x, (8, 128))

        @pl.loop(0, layers)
        def _(l):
            for k, c, at in ((W, 0, 0), (E, 128 // CH - 1, CH - 1)):
                rows = slice(c * CH, c * CH + CH)
                for h in range(2):
                    cols = slice(h * 128, h * 128 + 128)
                    hv = jnp.broadcast_to(row(k, l, h), (CH, 128))
                    add = tt[k, l, rows, cols].astype(F32) * hv * rdiag[f, l, rows, cols]
                    dst[nxt, 2 * l + h, rows, :] += jnp.where(subc == at, add, 0.0)
            for k, h, at in ((S, 0, 0), (N, 1, 127)):
                cols = slice(h * 128, h * 128 + 128)
                hrow = col(k, l)
                for c in range(128 // CH):
                    rows = slice(c * CH, c * CH + CH)
                    hv = jnp.concatenate(
                        [lane_pick(hrow, sub8 + (c * CH + 8 * i)) for i in range(CH // 8)], axis=0
                    )
                    add = tt[k, l, rows, cols].astype(F32) * hv * rdiag[f, l, rows, cols]
                    dst[nxt, 2 * l + h, rows, :] += jnp.where(lanec == at, add, 0.0)

    def sample(nxt):
        flat = pbuf.at[nxt].reshape(2 * layers * 128, 128)

        @pl.loop(0, blocks)
        def _(q):
            acc = jnp.zeros((8, 128), F32)
            for g in range(16):
                blk = jnp.zeros((8, 128), F32)
                for i in range(8):
                    x = flat[pl.ds(row_idx[q, 8 * g + i], 1), :]
                    blk = jnp.where(sub8 == i, jnp.broadcast_to(x, (8, 128)), blk)
                at = lanes_r[pl.ds(pl.multiple_of(q * 128, 128) + 8 * g, 8), :]
                acc = jnp.where(lane8 == sub8 + 8 * g, lane_pick(blk, at), acc)
            samp[pl.ds(q, 1), :] = jnp.sum(acc, axis=0, keepdims=True)

    def partial_sums():
        tile = jnp.zeros((8, 128), F32)
        for q in range(blocks):
            x = jnp.broadcast_to(samp[q : q + 1, :], (segs, 128)) * coef[q].astype(F32)
            for j in range(groups):
                col = jnp.sum(x[8 * j : 8 * j + 8, :], axis=1, keepdims=True)
                tile = jnp.where(lane8 == blocks * j + q, jnp.broadcast_to(col, (8, 128)), tile)
        return tile

    def corrections(it):
        for q in range(blocks):
            acc = jnp.zeros((8, 128), F32)
            for d in range(n_gy):
                acc = acc + jnp.where(wall[d] == well_s[q], ag[it, d], 0.0)
            tot = jnp.zeros((8, 128), F32)
            for j in range(groups):
                mine = jnp.where(lane8 // blocks == j, acc, 0.0)
                col = jnp.sum(mine, axis=1, keepdims=True)
                tot = tot + kmat[q, 8 * j : 8 * j + 8, :] * col
            corr[q : q + 1, :] = jnp.sum(tot, axis=0, keepdims=True)

    def scatter(nxt):
        ib = lax.broadcasted_iota(jnp.int32, (32, 128), 0)

        @pl.loop(0, 256 // 32)
        def _(i):
            for q in range(blocks):
                b = jnp.bitwise_and(cells[q : q + 1, :], 255)
                c = corr[q : q + 1, :]
                hi = c.astype(BF16).astype(F32)
                lo = c - hi
                hit = ib + i * 32 == b
                at = pl.ds(pl.multiple_of(i * 32, 32), 32)
                at2 = pl.ds(pl.multiple_of(i * 32 + 256, 32), 32)
                cvt[at, q * 128 : q * 128 + 128] = jnp.where(hit, hi, 0.0).astype(BF16)
                cvt[at2, q * 128 : q * 128 + 128] = jnp.where(hit, lo, 0.0).astype(BF16)

        @pl.loop(0, layers)
        def _(l):
            r = lax.dot_general(
                ut[pl.ds(pl.multiple_of(l * 128, 128), 128), :],
                cvt[...],
                (((1,), (1,)), ((), ())),
                preferred_element_type=F32,
            )
            for h in range(2):
                pbuf[nxt, 2 * l + h] -= (
                    r[:, h * 128 : h * 128 + 128] + r[:, 256 + h * 128 : 256 + h * 128 + 128]
                )

    @pl.loop(0, ITERS)
    def _(it):
        par = lax.rem(it, 2)
        nxt = 1 - par
        p_inner(par, nxt)
        halo_wait(it, 0)
        add_halo(it, 0, trans, pbuf, nxt)
        sample(nxt)
        tile = partial_sums()
        agsend[it] = tile
        ag[it, gy] = tile
        for d in range(1, n_gy):
            peer_copy(agsend.at[it], ag.at[it, gy], ss_ag.at[it, d - 1], rs_ag.at[it, gy], d).start()
        s_inner(par, nxt)
        halo_wait(it, 1)
        add_halo(it, 1, tu, sbuf, nxt)

        @pl.when(it < ITERS - 1)
        def _():
            halo_send(sbuf, nxt, it + 1, 1)

        for d in range(1, n_gy):
            peer = lax.rem(gy + d, n_gy)
            peer_copy(
                agsend.at[it], ag.at[it, peer], ss_ag.at[it, d - 1], rs_ag.at[it, peer], d
            ).wait_recv()
        corrections(it)
        scatter(nxt)

        @pl.when(it < ITERS - 1)
        def _():
            halo_send(pbuf, nxt, it + 1, 0)

    last = ITERS % 2
    for l in range(layers):
        for h in range(2):
            out[0, l, :, h * 128 : h * 128 + 128] = pbuf[last, 2 * l + h]
            out[1, l, :, h * 128 : h * 128 + 128] = sbuf[last, 2 * l + h]

    for d in range(1, n_gy):
        peer_copy(wsend, wall.at[gy], ss_w.at[d - 1], rs_w.at[gy], d).wait_send()
        for it in range(ITERS):
            peer_copy(
                agsend.at[it], ag.at[it, gy], ss_ag.at[it, d - 1], rs_ag.at[it, gy], d
            ).wait_send()
    for k in (W, E, S, N):

        @pl.when(there[k])
        def _():
            for it in range(ITERS):
                for f in range(2):
                    halo_copy(it, f, k, k).wait_send()


def shards(
    n_gx,
    n_gy,
    source,
    transmissibility,
    diagonal,
    upwind_flags,
    panel_coef,
    perf_cell,
    panel_well,
    seg_count,
    well_inverse,
):
    layers = upwind_flags.shape[0]
    cell = perf_cell[0, 0]
    row_idx = (
        jnp.left_shift(jnp.right_shift(cell, 15), 8)
        + jnp.left_shift(jnp.bitwise_and(jnp.right_shift(cell, 7), 1), 7)
        + jnp.bitwise_and(jnp.right_shift(cell, 8), 127)
    )
    vmem = pl.BlockSpec(memory_space=pltpu.VMEM)
    smem = pl.BlockSpec(memory_space=pltpu.SMEM)
    dma = pltpu.SemaphoreType.DMA
    blocks, segs = panel_coef.shape[2:4]
    rows = blocks * 128
    return pl.pallas_call(
        functools.partial(kernel, n_gx, n_gy),
        out_shape=jax.ShapeDtypeStruct(source.shape, F32),
        in_specs=[smem] * 3 + [vmem] * 7,
        out_specs=vmem,
        scratch_shapes=[
            pltpu.VMEM((2, 2 * layers, 128, 128), F32),
            pltpu.VMEM((2, 2 * layers, 128, 128), F32),
            pltpu.VMEM(transmissibility.shape, BF16),
            pltpu.VMEM(diagonal.shape, F32),
            pltpu.VMEM((layers * 128, rows), BF16),
            pltpu.VMEM((512, rows), BF16),
            pltpu.VMEM((8, 128), F32),
            pltpu.VMEM((rows, 128), jnp.int32),
            pltpu.VMEM((blocks, segs, 128), F32),
            pltpu.VMEM((blocks, 128), F32),
            pltpu.VMEM((blocks, 128), F32),
            pltpu.VMEM((ITERS, 2, 2, 2 * layers, 128), F32),
            pltpu.VMEM((ITERS, 2, 2, 2 * layers, 128), F32),
            pltpu.VMEM((ITERS, 2, 2, layers, 128), F32),
            pltpu.VMEM((ITERS, 2, 2, layers, 128), F32),
            pltpu.VMEM((8, 128), jnp.int32),
            pltpu.VMEM((n_gy, 8, 128), jnp.int32),
            pltpu.VMEM((ITERS, 8, 128), F32),
            pltpu.VMEM((ITERS, n_gy, 8, 128), F32),
            dma((ITERS, 2, 2)),
            dma((ITERS, 2, 2)),
            dma((ITERS, 2, 2)),
            dma((ITERS, 2, 2)),
            dma((n_gy - 1,)),
            dma((n_gy,)),
            dma((ITERS, n_gy - 1)),
            dma((ITERS, n_gy)),
        ],
        compiler_params=pltpu.CompilerParams(
            collective_id=0, has_side_effects=True, vmem_limit_bytes=60 * 1024 * 1024
        ),
    )(
        row_idx,
        panel_well[0, 0],
        seg_count[0],
        source,
        transmissibility,
        diagonal,
        upwind_flags,
        panel_coef[0, 0],
        cell,
        well_inverse[0],
    )


def solution(mesh):
    placed = (
        P(None, None, "gx", "gy"),
        P(None, None, "gx", "gy"),
        P(None, None, "gx", "gy"),
        P(None, "gx", "gy"),
        P("gx", "gy", None, None, None),
        P("gx", "gy", None, None),
        P("gx", "gy", None),
        P("gx", None),
        P("gx", None, None, None),
    )
    return jax.shard_map(
        functools.partial(shards, mesh.shape["gx"], mesh.shape["gy"]),
        mesh=mesh,
        in_specs=placed,
        out_specs=P(None, None, "gx", "gy"),
        check_vma=False,
    )
```

```python
import functools

import jax
import jax.numpy as jnp
from jax import lax
from jax.experimental import pallas as pl
from jax.experimental.pallas import tpu as pltpu
from jax.sharding import PartitionSpec as P

ITERS = 3
MESH = pl.DeviceIdType.MESH
F32 = jnp.float32
BF16 = jnp.bfloat16
W, E, S, N = 0, 1, 2, 3
CH = 16


def lane_pick(x, idx):
    return jnp.take_along_axis(x, idx, axis=1, mode="promise_in_bounds")


def kernel(
    n_gx,
    n_gy,
    well_s,
    count_s,
    src_h,
    trans_h,
    diag_h,
    flags_h,
    coef_h,
    cells_h,
    inv_h,
    out_h,
    p_src,
    s_src,
    p_a,
    p_b,
    s_a,
    s_b,
    trans,
    flags,
    rdiag,
    tu,
    coef,
    cells,
    inv,
    ut,
    vt,
    cvt,
    out_p,
    lanes_r,
    row_v,
    row_idx,
    kmat,
    samp,
    corr,
    srow,
    rrow,
    scol,
    rcol,
    wsend,
    wall,
    agsend,
    ag,
    ld,
    ss_row,
    rs_row,
    ss_col,
    rs_col,
    ss_w,
    rs_w,
    ss_ag,
    rs_ag,
):
    gx = lax.axis_index("gx")
    gy = lax.axis_index("gy")
    there = (gx > 0, gx < n_gx - 1, gy > 0, gy < n_gy - 1)
    peer_id = ({"gx": gx - 1}, {"gx": gx + 1}, {"gy": gy - 1}, {"gy": gy + 1})
    layers = trans.shape[1]
    blocks = coef.shape[0]
    segs = coef.shape[1]
    groups = segs // 8
    halves = (slice(0, 128), slice(128, 256))

    sub8 = lax.broadcasted_iota(jnp.int32, (8, 128), 0)
    lane8 = lax.broadcasted_iota(jnp.int32, (8, 128), 1)
    subc = lax.broadcasted_iota(jnp.int32, (CH, 128), 0)
    lanec = lax.broadcasted_iota(jnp.int32, (CH, 128), 1)

    def half_of(ref, h):
        return ref.reshape(layers, 2, 128, 128).at[:, h]

    loads = [
        pltpu.make_async_copy(src_h.at[f, :, :, halves[h]], half_of(ref, h), ld.at[2 * f + h])
        for f, ref in enumerate((p_src, s_src))
        for h in range(2)
    ]
    load_cells = pltpu.make_async_copy(cells_h, cells, ld.at[4])
    load_coef = pltpu.make_async_copy(coef_h, coef, ld.at[5])
    load_inv = pltpu.make_async_copy(inv_h, inv, ld.at[6])
    load_dp = pltpu.make_async_copy(diag_h.at[0], rdiag.at[0], ld.at[7])
    load_ds = pltpu.make_async_copy(diag_h.at[1], rdiag.at[1], ld.at[8])
    load_t = pltpu.make_async_copy(trans_h, trans, ld.at[9])
    load_f = pltpu.make_async_copy(flags_h, flags, ld.at[10])
    load_cells.start()
    for x in loads:
        x.start()
    for x in (load_coef, load_inv, load_dp, load_t, load_ds, load_f):
        x.start()

    barrier = pltpu.get_barrier_semaphore()
    for d in range(1, n_gy):
        pl.semaphore_signal(
            barrier, inc=1, device_id={"gy": lax.rem(gy + d, n_gy)}, device_id_type=MESH
        )
    for k in (W, E):

        @pl.when(there[k])
        def _():
            pl.semaphore_signal(barrier, inc=1, device_id=peer_id[k], device_id_type=MESH)

    def halo_copy(it, f, k, dst_side):
        if k in (W, E):
            return pltpu.make_async_remote_copy(
                src_ref=srow.at[it, f, k],
                dst_ref=rrow.at[it, f, dst_side],
                send_sem=ss_row.at[it, f, k],
                recv_sem=rs_row.at[it, f, dst_side],
                device_id=peer_id[k],
                device_id_type=MESH,
            )
        return pltpu.make_async_remote_copy(
            src_ref=scol.at[it, f, k - 2],
            dst_ref=rcol.at[it, f, dst_side - 2],
            send_sem=ss_col.at[it, f, k - 2],
            recv_sem=rs_col.at[it, f, dst_side - 2],
            device_id=peer_id[k],
            device_id_type=MESH,
        )

    def halo_pack(buf, it, f):
        srow[it, f, W] = buf[:, 0, :]
        srow[it, f, E] = buf[:, 127, :]

        def one(l):
            for side, half, lane in ((0, 0, 0), (1, 1, 127)):
                acc = jnp.zeros((8, 128), F32)
                for g in range(16):
                    v = buf[2 * l + half, 8 * g : 8 * g + 8, :]
                    b = jnp.broadcast_to(v[:, lane : lane + 1], (8, 128))
                    acc = jnp.where(lane8 == sub8 + 8 * g, b, acc)
                scol[it, f, side, pl.ds(l, 1), :] = jnp.sum(acc, axis=0, keepdims=True)

        pl.loop(0, layers, unroll=4)(one)

    def halo_start(it, f):
        for k in (S, N, W, E):

            @pl.when(there[k])
            def _():
                halo_copy(it, f, k, 1 - k if k < 2 else 5 - k).start()

    def halo_wait(it, f):
        for k in (W, E, S, N):

            @pl.when(there[k])
            def _():
                halo_copy(it, f, k, k).wait_recv()

    def peer_copy(src_ref, dst_ref, send_sem, recv_sem, d):
        return pltpu.make_async_remote_copy(
            src_ref=src_ref,
            dst_ref=dst_ref,
            send_sem=send_sem,
            recv_sem=recv_sem,
            device_id={"gy": lax.rem(gy + d, n_gy)},
            device_id_type=MESH,
        )

    wrow = jnp.zeros((8, 128), jnp.int32)
    for q in range(blocks):
        wrow = jnp.where(lax.rem(lane8, blocks) == q, well_s[q], wrow)
    wsend[...] = wrow
    wall[gy] = wrow

    load_cells.wait()
    cell = cells[...]
    row_v[...] = (
        jnp.left_shift(jnp.right_shift(cell, 15), 8)
        + jnp.left_shift(jnp.bitwise_and(jnp.right_shift(cell, 7), 1), 7)
        + jnp.bitwise_and(jnp.right_shift(cell, 8), 127)
    )
    load_rows = pltpu.make_async_copy(row_v, row_idx, ld.at[11])
    load_rows.start()

    for x in loads:
        x.wait()
    halo_pack(p_src, 0, 0)
    halo_pack(s_src, 0, 1)

    beside = jnp.where(there[W], 1, 0) + jnp.where(there[E], 1, 0)
    pl.semaphore_wait(barrier, n_gy - 1 + beside)
    halo_start(0, 0)
    halo_start(0, 1)
    for d in range(1, n_gy):
        peer_copy(wsend, wall.at[gy], ss_w.at[d - 1], rs_w.at[gy], d).start()

    for k in (W, E):

        @pl.when(jnp.logical_not(there[k]))
        def _():
            for it in range(ITERS):
                for f in range(2):
                    rrow[it, f, k] = jnp.zeros((16, 128), F32)

    for k in (S, N):

        @pl.when(jnp.logical_not(there[k]))
        def _():
            for it in range(ITERS):
                for f in range(2):
                    rcol[it, f, k - 2] = jnp.zeros((8, 128), F32)

    def lanes_of(q):
        lane = jnp.broadcast_to(jnp.bitwise_and(cells[pl.ds(q, 1), :], 127), (128, 128))
        lanes_r[pl.ds(pl.multiple_of(q * 128, 128), 128), :] = lane.T

    pl.loop(0, blocks, unroll=2)(lanes_of)

    def hot_rows(i):
        i32 = lax.broadcasted_iota(jnp.int32, (32, 128), 0) + i * 32
        for q in range(blocks):
            a = jnp.right_shift(cells[q : q + 1, :], 8)
            hot = jnp.where(i32 == a, 1.0, 0.0).astype(BF16)
            ut[pl.ds(pl.multiple_of(i * 32, 32), 32), q * 128 : q * 128 + 128] = hot

    pl.loop(0, ut.shape[0] // 32, unroll=2)(hot_rows)

    def hot_cols(i):
        i32 = lax.broadcasted_iota(jnp.int32, (32, 128), 0) + i * 32
        for q in range(blocks):
            b = jnp.bitwise_and(cells[q : q + 1, :], 255)
            hot = jnp.where(i32 == b, 1.0, 0.0).astype(BF16)
            vt[pl.ds(pl.multiple_of(i * 32, 32), 32), q * 128 : q * 128 + 128] = hot

    pl.loop(0, vt.shape[0] // 32, unroll=2)(hot_cols)

    def make_kmat():
        i0 = lax.broadcasted_iota(jnp.int32, (segs, segs), 0)
        i1 = lax.broadcasted_iota(jnp.int32, (segs, segs), 1)

        def one(q):
            w = well_s[q]
            count = count_s[w]
            m = jnp.where(jnp.logical_and(i0 < count, i1 < count), inv[w], 0.0)
            kmat[q] = lax.dot_general(
                m,
                coef[q].astype(F32),
                (((0,), (0,)), ((), ())),
                precision=lax.Precision.HIGHEST,
                preferred_element_type=F32,
            )

        pl.loop(0, blocks, unroll=2)(one)

    def invert(f):
        def one(l):
            rdiag[f, l] = 1.0 / rdiag[f, l]

        pl.loop(0, layers)(one)

    def make_tu():
        def one(l):
            for c in range(128 // CH):
                rows = slice(c * CH, c * CH + CH)
                fl = flags[l, rows, :]
                for k in range(4):
                    bit = jnp.bitwise_and(jnp.right_shift(fl, k), 1)
                    t = trans[k, l, rows, :].astype(F32)
                    tu[k, l, rows, :] = jnp.where(bit == 1, t, 0.0).astype(BF16)

        pl.loop(0, layers)(one)

    def col_of(hrow, c):
        return jnp.concatenate(
            [lane_pick(hrow, sub8 + (c * CH + 8 * i)) for i in range(CH // 8)], axis=0
        )

    def neighbours(load, c, west_row, east_row, south_col, north_col):
        r0 = c * CH
        mid = [load(h, r0) for h in range(2)]
        if c == 0:
            west = [jnp.where(subc == 0, west_row[h], pltpu.roll(mid[h], 1, 0)) for h in range(2)]
        else:
            west = [load(h, r0 - 1) for h in range(2)]
        if c == 128 // CH - 1:
            east = [
                jnp.where(subc == CH - 1, east_row[h], pltpu.roll(mid[h], CH - 1, 0))
                for h in range(2)
            ]
        else:
            east = [load(h, r0 + 1) for h in range(2)]
        up = [pltpu.roll(x, 1, 1) for x in mid]
        down = [pltpu.roll(x, 127, 1) for x in mid]
        south = [jnp.where(lanec == 0, south_col, up[0]), jnp.where(lanec == 0, up[0], up[1])]
        north = [
            jnp.where(lanec == 127, down[1], down[0]),
            jnp.where(lanec == 127, north_col, down[1]),
        ]
        return west, east, south, north

    def p_inner(old, new):
        def one(l):
            for c in range(128 // CH):
                rows = slice(c * CH, c * CH + CH)
                near = neighbours(
                    lambda h, r: old[2 * l + h, r : r + CH, :], c, (0.0, 0.0), (0.0, 0.0), 0.0, 0.0
                )
                for h in range(2):
                    acc = p_src[2 * l + h, rows, :]
                    for k in range(4):
                        acc = acc + trans[k, l, rows, halves[h]].astype(F32) * near[k][h]
                    new[2 * l + h, rows, :] = acc * rdiag[0, l, rows, halves[h]]

        pl.loop(0, layers, unroll=2)(one)

    def p_halo(it, new):
        def one(l):
            for k, c, at in ((W, 0, 0), (E, 128 // CH - 1, CH - 1)):
                rows = slice(c * CH, c * CH + CH)
                for h in range(2):
                    hv = jnp.broadcast_to(rrow[it, 0, k, pl.ds(2 * l + h, 1), :], (CH, 128))
                    t = trans[k, l, rows, halves[h]].astype(F32)
                    add = t * hv * rdiag[0, l, rows, halves[h]]
                    new[2 * l + h, rows, :] += jnp.where(subc == at, add, 0.0)
            for k, h, at in ((S, 0, 0), (N, 1, 127)):
                hrow = jnp.broadcast_to(rcol[it, 0, k - 2, pl.ds(l, 1), :], (8, 128))
                for c in range(128 // CH):
                    rows = slice(c * CH, c * CH + CH)
                    t = trans[k, l, rows, halves[h]].astype(F32)
                    add = t * col_of(hrow, c) * rdiag[0, l, rows, halves[h]]
                    new[2 * l + h, rows, :] += jnp.where(lanec == at, add, 0.0)

        pl.loop(0, layers, unroll=2)(one)

    def s_sweep(it, oldp, olds, store):
        def one(l):
            def row(k, h):
                at = pl.ds(2 * l + h, 1)
                return rrow[it, 1, k, at, :] + 0.3 * rrow[it, 0, k, at, :]

            def col(k):
                at = pl.ds(l, 1)
                x = rcol[it, 1, k - 2, at, :] + 0.3 * rcol[it, 0, k - 2, at, :]
                return jnp.broadcast_to(x, (8, 128))

            west_row = [row(W, h) for h in range(2)]
            east_row = [row(E, h) for h in range(2)]
            south, north = col(S), col(N)
            for c in range(128 // CH):
                rows = slice(c * CH, c * CH + CH)
                near = neighbours(
                    lambda h, r: olds[2 * l + h, r : r + CH, :] + 0.3 * oldp[2 * l + h, r : r + CH, :],
                    c,
                    west_row,
                    east_row,
                    col_of(south, c),
                    col_of(north, c),
                )
                for h in range(2):
                    acc = s_src[2 * l + h, rows, :]
                    p3 = 0.3 * oldp[2 * l + h, rows, :]
                    for k in range(4):
                        acc = acc + tu[k, l, rows, halves[h]].astype(F32) * (near[k][h] - p3)
                    store(l, h, rows, acc * rdiag[1, l, rows, halves[h]])

        pl.loop(0, layers, unroll=2)(one)

    def sample(new):
        flat = new.reshape(2 * layers * 128, 128)

        def one(q):
            acc = jnp.zeros((8, 128), F32)
            for g in range(16):
                blk = jnp.zeros((8, 128), F32)
                for i in range(8):
                    x = flat[pl.ds(row_idx[q, 8 * g + i], 1), :]
                    blk = jnp.where(sub8 == i, jnp.broadcast_to(x, (8, 128)), blk)
                at = lanes_r[pl.ds(pl.multiple_of(q * 128, 128) + 8 * g, 8), :]
                acc = jnp.where(lane8 == sub8 + 8 * g, lane_pick(blk, at), acc)
            samp[pl.ds(q, 1), :] = jnp.sum(acc, axis=0, keepdims=True)

        pl.loop(0, blocks, unroll=4)(one)

    def partial_sums():
        tile = jnp.zeros((8, 128), F32)
        for q in range(blocks):
            x = jnp.broadcast_to(samp[q : q + 1, :], (segs, 128)) * coef[q].astype(F32)
            for j in range(groups):
                col = jnp.sum(x[8 * j : 8 * j + 8, :], axis=1, keepdims=True)
                tile = jnp.where(lane8 == blocks * j + q, jnp.broadcast_to(col, (8, 128)), tile)
        return tile

    def corrections(it):
        for q in range(blocks):
            acc = jnp.zeros((8, 128), F32)
            for d in range(n_gy):
                acc = acc + jnp.where(wall[d] == well_s[q], ag[it, d], 0.0)
            tot = jnp.zeros((8, 128), F32)
            for j in range(groups):
                mine = jnp.where(lane8 // blocks == j, acc, 0.0)
                col = jnp.sum(mine, axis=1, keepdims=True)
                tot = tot + kmat[q, 8 * j : 8 * j + 8, :] * col
            corr[q : q + 1, :] = jnp.sum(tot, axis=0, keepdims=True)

    def scatter(new, store):
        def one(i):
            at = pl.ds(pl.multiple_of(i * 32, 32), 32)
            at2 = pl.ds(pl.multiple_of(i * 32 + 256, 32), 32)
            for q in range(blocks):
                c = corr[q : q + 1, :]
                hi = c.astype(BF16)
                lo = (c - hi.astype(F32)).astype(BF16)
                v = vt[at, q * 128 : q * 128 + 128]
                cvt[at, q * 128 : q * 128 + 128] = v * hi
                cvt[at2, q * 128 : q * 128 + 128] = v * lo

        pl.loop(0, 256 // 32, unroll=2)(one)
        r = lax.dot_general(
            ut[...], cvt[...], (((1,), (1,)), ((), ())), preferred_element_type=F32
        )
        for l in range(layers):
            at = slice(l * 128, l * 128 + 128)
            for h in range(2):
                both = r[at, halves[h]] + r[at, 256 + h * 128 : 384 + h * 128]
                store(l, h, new[2 * l + h] - both)

    old_p, old_s = p_src, s_src
    spare = ((p_a, s_a), (p_b, s_b), (p_a, s_a))
    for it in range(ITERS):
        new_p, new_s = spare[it]
        if it == 0:
            load_dp.wait()
            load_t.wait()
            invert(0)
        p_inner(old_p, new_p)
        if it == 0:
            load_rows.wait()
            load_coef.wait()
        halo_wait(it, 0)
        p_halo(it, new_p)
        sample(new_p)
        tile = partial_sums()
        agsend[it] = tile
        ag[it, gy] = tile
        for d in range(1, n_gy):
            peer_copy(agsend.at[it], ag.at[it, gy], ss_ag.at[it, d - 1], rs_ag.at[it, gy], d).start()
        if it == 0:
            load_ds.wait()
            load_f.wait()
            invert(1)
            make_tu()
            load_inv.wait()
            make_kmat()
            for d in range(1, n_gy):
                peer = lax.rem(gy + d, n_gy)
                peer_copy(wsend, wall.at[peer], ss_w.at[d - 1], rs_w.at[peer], d).wait_recv()
        halo_wait(it, 1)

        def keep_s(l, h, rows, x):
            new_s[2 * l + h, rows, :] = x

        def last_s(l, h, rows, x):
            out_p[1, l, rows, halves[h]] = x

        s_sweep(it, old_p, old_s, keep_s if it < ITERS - 1 else last_s)
        if it < ITERS - 1:
            halo_pack(new_s, it + 1, 1)
            halo_start(it + 1, 1)
        else:
            save_s = pltpu.make_async_copy(out_p.at[1], out_h.at[1], ld.at[0])
            save_s.start()
        for d in range(1, n_gy):
            peer = lax.rem(gy + d, n_gy)
            peer_copy(
                agsend.at[it], ag.at[it, peer], ss_ag.at[it, d - 1], rs_ag.at[it, peer], d
            ).wait_recv()
        corrections(it)

        def keep_p(l, h, x):
            new_p[2 * l + h] = x

        def last_p(l, h, x):
            out_p[0, l, :, halves[h]] = x

        scatter(new_p, keep_p if it < ITERS - 1 else last_p)
        if it < ITERS - 1:
            halo_pack(new_p, it + 1, 0)
            halo_start(it + 1, 0)
        old_p, old_s = new_p, new_s

    save_p = pltpu.make_async_copy(out_p.at[0], out_h.at[0], ld.at[1])
    save_p.start()
    for d in range(1, n_gy):
        peer_copy(wsend, wall.at[gy], ss_w.at[d - 1], rs_w.at[gy], d).wait_send()
        for it in range(ITERS):
            peer_copy(
                agsend.at[it], ag.at[it, gy], ss_ag.at[it, d - 1], rs_ag.at[it, gy], d
            ).wait_send()
    for k in (W, E, S, N):

        @pl.when(there[k])
        def _():
            for it in range(ITERS):
                for f in range(2):
                    halo_copy(it, f, k, k).wait_send()

    save_s.wait()
    save_p.wait()


def shards(
    n_gx,
    n_gy,
    source,
    transmissibility,
    diagonal,
    upwind_flags,
    panel_coef,
    perf_cell,
    panel_well,
    seg_count,
    well_inverse,
):
    layers = upwind_flags.shape[0]
    anywhere = pl.BlockSpec(memory_space=pl.ANY)
    smem = pl.BlockSpec(memory_space=pltpu.SMEM)
    dma = pltpu.SemaphoreType.DMA
    blocks, segs = panel_coef.shape[2:4]
    rows = blocks * 128
    field = pltpu.VMEM((2 * layers, 128, 128), F32)
    return pl.pallas_call(
        functools.partial(kernel, n_gx, n_gy),
        out_shape=jax.ShapeDtypeStruct(source.shape, F32),
        in_specs=[smem] * 2 + [anywhere] * 7,
        out_specs=anywhere,
        scratch_shapes=[
            field,
            field,
            field,
            field,
            field,
            field,
            pltpu.VMEM(transmissibility.shape, BF16),
            pltpu.VMEM(upwind_flags.shape, jnp.int32),
            pltpu.VMEM(diagonal.shape, F32),
            pltpu.VMEM(transmissibility.shape, BF16),
            pltpu.VMEM((blocks, segs, 128), BF16),
            pltpu.VMEM((blocks, 128), jnp.int32),
            pltpu.VMEM(well_inverse.shape[1:], F32),
            pltpu.VMEM((layers * 128, rows), BF16),
            pltpu.VMEM((256, rows), BF16),
            pltpu.VMEM((512, rows), BF16),
            pltpu.VMEM(source.shape, F32),
            pltpu.VMEM((rows, 128), jnp.int32),
            pltpu.VMEM((blocks, 128), jnp.int32),
            pltpu.SMEM((blocks, 128), jnp.int32),
            pltpu.VMEM((blocks, segs, 128), F32),
            pltpu.VMEM((blocks, 128), F32),
            pltpu.VMEM((blocks, 128), F32),
            pltpu.VMEM((ITERS, 2, 2, 2 * layers, 128), F32),
            pltpu.VMEM((ITERS, 2, 2, 2 * layers, 128), F32),
            pltpu.VMEM((ITERS, 2, 2, layers, 128), F32),
            pltpu.VMEM((ITERS, 2, 2, layers, 128), F32),
            pltpu.VMEM((8, 128), jnp.int32),
            pltpu.VMEM((n_gy, 8, 128), jnp.int32),
            pltpu.VMEM((ITERS, 8, 128), F32),
            pltpu.VMEM((ITERS, n_gy, 8, 128), F32),
            dma((12,)),
            dma((ITERS, 2, 2)),
            dma((ITERS, 2, 2)),
            dma((ITERS, 2, 2)),
            dma((ITERS, 2, 2)),
            dma((n_gy - 1,)),
            dma((n_gy,)),
            dma((ITERS, n_gy - 1)),
            dma((ITERS, n_gy)),
        ],
        compiler_params=pltpu.CompilerParams(
            collective_id=0, has_side_effects=True, vmem_limit_bytes=56 * 1024 * 1024
        ),
    )(
        panel_well[0, 0],
        seg_count[0],
        source,
        transmissibility,
        diagonal,
        upwind_flags,
        panel_coef[0, 0],
        perf_cell[0, 0],
        well_inverse[0],
    )


def solution(mesh):
    placed = (
        P(None, None, "gx", "gy"),
        P(None, None, "gx", "gy"),
        P(None, None, "gx", "gy"),
        P(None, "gx", "gy"),
        P("gx", "gy", None, None, None),
        P("gx", "gy", None, None),
        P("gx", "gy", None),
        P("gx", None),
        P("gx", None, None, None),
    )
    return jax.shard_map(
        functools.partial(shards, mesh.shape["gx"], mesh.shape["gy"]),
        mesh=mesh,
        in_specs=placed,
        out_specs=P(None, None, "gx", "gy"),
        check_vma=False,
    )
```

```python
import functools

import jax
import jax.numpy as jnp
from jax import lax
from jax.experimental import pallas as pl
from jax.experimental.pallas import tpu as pltpu
from jax.sharding import PartitionSpec as P

ITERS = 3
MESH = pl.DeviceIdType.MESH
F32 = jnp.float32
BF16 = jnp.bfloat16
W, E, S, N = 0, 1, 2, 3
CH = 16
MM = 512


def lane_pick(x, idx):
    return jnp.take_along_axis(x, idx, axis=1, mode="promise_in_bounds")


def kernel(
    n_gx,
    n_gy,
    well_s,
    count_s,
    src_h,
    trans_h,
    diag_h,
    flags_h,
    coef_h,
    cells_h,
    inv_h,
    out_h,
    p_src,
    s_src,
    p_a,
    p_b,
    s_a,
    s_b,
    trans,
    flags,
    rdiag,
    tu,
    coef,
    cells,
    inv,
    ut,
    vt,
    cvt,
    ut_edge,
    edge,
    wrows,
    wcols,
    out_p,
    lanes_r,
    row_v,
    row_idx,
    kmat,
    samp,
    corr,
    srow,
    rrow,
    scol,
    rcol,
    wsend,
    wall,
    agsend,
    ag,
    ld,
    ss_row,
    rs_row,
    ss_col,
    rs_col,
    ss_w,
    rs_w,
    ss_ag,
    rs_ag,
):
    gx = lax.axis_index("gx")
    gy = lax.axis_index("gy")
    there = (gx > 0, gx < n_gx - 1, gy > 0, gy < n_gy - 1)
    peer_id = ({"gx": gx - 1}, {"gx": gx + 1}, {"gy": gy - 1}, {"gy": gy + 1})
    layers = trans.shape[1]
    blocks = coef.shape[0]
    segs = coef.shape[1]
    groups = segs // 8
    halves = (slice(0, 128), slice(128, 256))

    sub8 = lax.broadcasted_iota(jnp.int32, (8, 128), 0)
    lane8 = lax.broadcasted_iota(jnp.int32, (8, 128), 1)
    subc = lax.broadcasted_iota(jnp.int32, (CH, 128), 0)
    lanec = lax.broadcasted_iota(jnp.int32, (CH, 128), 1)

    def half_of(ref, h):
        return ref.reshape(layers, 2, 128, 128).at[:, h]

    loads = [
        pltpu.make_async_copy(src_h.at[f, :, :, halves[h]], half_of(ref, h), ld.at[2 * f + h])
        for f, ref in enumerate((p_src, s_src))
        for h in range(2)
    ]
    load_cells = pltpu.make_async_copy(cells_h, cells, ld.at[4])
    load_coef = pltpu.make_async_copy(coef_h, coef, ld.at[5])
    load_inv = pltpu.make_async_copy(inv_h, inv, ld.at[6])
    load_dp = pltpu.make_async_copy(diag_h.at[0], rdiag.at[0], ld.at[7])
    load_ds = pltpu.make_async_copy(diag_h.at[1], rdiag.at[1], ld.at[8])
    load_t = pltpu.make_async_copy(trans_h, trans, ld.at[9])
    load_f = pltpu.make_async_copy(flags_h, flags, ld.at[10])
    load_cells.start()
    for x in loads:
        x.start()
    for x in (load_coef, load_inv, load_dp, load_t, load_ds, load_f):
        x.start()

    barrier = pltpu.get_barrier_semaphore()
    for d in range(1, n_gy):
        pl.semaphore_signal(
            barrier, inc=1, device_id={"gy": lax.rem(gy + d, n_gy)}, device_id_type=MESH
        )
    for k in (W, E):

        @pl.when(there[k])
        def _():
            pl.semaphore_signal(barrier, inc=1, device_id=peer_id[k], device_id_type=MESH)

    def halo_copy(it, f, k, dst_side):
        if k in (W, E):
            return pltpu.make_async_remote_copy(
                src_ref=srow.at[it, f, k],
                dst_ref=rrow.at[it, f, dst_side],
                send_sem=ss_row.at[it, f, k],
                recv_sem=rs_row.at[it, f, dst_side],
                device_id=peer_id[k],
                device_id_type=MESH,
            )
        return pltpu.make_async_remote_copy(
            src_ref=scol.at[it, f, k - 2],
            dst_ref=rcol.at[it, f, dst_side - 2],
            send_sem=ss_col.at[it, f, k - 2],
            recv_sem=rs_col.at[it, f, dst_side - 2],
            device_id=peer_id[k],
            device_id_type=MESH,
        )

    def halo_pack(buf, it, f):
        for h in range(2):
            for k, r in ((W, 0), (E, 127)):
                srow[it, f, k, h * layers : h * layers + layers] = half_of(buf, h)[:, r, :]

        def one(l):
            for side, half, lane in ((0, 0, 0), (1, 1, 127)):
                acc = jnp.zeros((8, 128), F32)
                for g in range(16):
                    v = buf[2 * l + half, 8 * g : 8 * g + 8, :]
                    b = jnp.broadcast_to(v[:, lane : lane + 1], (8, 128))
                    acc = jnp.where(lane8 == sub8 + 8 * g, b, acc)
                scol[it, f, side, pl.ds(l, 1), :] = jnp.sum(acc, axis=0, keepdims=True)

        pl.loop(0, layers, unroll=4)(one)

    def halo_start(it, f):
        for k in (S, N, W, E):

            @pl.when(there[k])
            def _():
                halo_copy(it, f, k, 1 - k if k < 2 else 5 - k).start()

    def halo_wait(it, f, sides=(W, E, S, N)):
        for k in sides:

            @pl.when(there[k])
            def _():
                halo_copy(it, f, k, k).wait_recv()

    def peer_copy(src_ref, dst_ref, send_sem, recv_sem, d):
        return pltpu.make_async_remote_copy(
            src_ref=src_ref,
            dst_ref=dst_ref,
            send_sem=send_sem,
            recv_sem=recv_sem,
            device_id={"gy": lax.rem(gy + d, n_gy)},
            device_id_type=MESH,
        )

    wrow = jnp.zeros((8, 128), jnp.int32)
    for q in range(blocks):
        wrow = jnp.where(lax.rem(lane8, blocks) == q, well_s[q], wrow)
    wsend[...] = wrow
    wall[gy] = wrow

    load_cells.wait()
    cell = cells[...]
    row_v[...] = (
        jnp.left_shift(jnp.right_shift(cell, 15), 8)
        + jnp.left_shift(jnp.bitwise_and(jnp.right_shift(cell, 7), 1), 7)
        + jnp.bitwise_and(jnp.right_shift(cell, 8), 127)
    )
    load_rows = pltpu.make_async_copy(row_v, row_idx, ld.at[11])
    load_rows.start()

    def lanes_of(q):
        lane = jnp.broadcast_to(jnp.bitwise_and(cells[pl.ds(q, 1), :], 127), (128, 128))
        lanes_r[pl.ds(pl.multiple_of(q * 128, 128), 128), :] = lane.T

    pl.loop(0, blocks, unroll=2)(lanes_of)

    def hot_rows(i):
        i32 = lax.broadcasted_iota(jnp.int32, (32, 128), 0) + i * 32
        for q in range(blocks):
            a = jnp.right_shift(cells[q : q + 1, :], 8)
            hot = jnp.where(i32 == a, 1.0, 0.0).astype(BF16)
            ut[pl.ds(pl.multiple_of(i * 32, 32), 32), q * 128 : q * 128 + 128] = hot

    pl.loop(0, ut.shape[0] // 32, unroll=2)(hot_rows)
    edge_row = lax.broadcasted_iota(jnp.int32, (16, 128), 0)
    edge_row = jnp.where(edge_row < layers, edge_row * 128, (edge_row - layers) * 128 + 127)
    for q in range(blocks):
        hit = edge_row == jnp.right_shift(cells[q : q + 1, :], 8)
        ut_edge[:, q * 128 : q * 128 + 128] = jnp.where(hit, 1.0, 0.0).astype(BF16)


    def hot_cols(i):
        i32 = lax.broadcasted_iota(jnp.int32, (32, 128), 0) + i * 32
        for q in range(blocks):
            b = jnp.bitwise_and(cells[q : q + 1, :], 255)
            hot = jnp.where(i32 == b, 1.0, 0.0).astype(BF16)
            vt[pl.ds(pl.multiple_of(i * 32, 32), 32), q * 128 : q * 128 + 128] = hot

    pl.loop(0, vt.shape[0] // 32, unroll=2)(hot_cols)

    for x in loads:
        x.wait()
    halo_pack(p_src, 0, 0)
    halo_pack(s_src, 0, 1)

    beside = jnp.where(there[W], 1, 0) + jnp.where(there[E], 1, 0)
    pl.semaphore_wait(barrier, n_gy - 1 + beside)
    halo_start(0, 0)
    halo_start(0, 1)
    for d in range(1, n_gy):
        peer_copy(wsend, wall.at[gy], ss_w.at[d - 1], rs_w.at[gy], d).start()

    for k in (W, E):

        @pl.when(jnp.logical_not(there[k]))
        def _():
            for it in range(ITERS):
                for f in range(2):
                    rrow[it, f, k] = jnp.zeros((16, 128), F32)

    for k in (S, N):

        @pl.when(jnp.logical_not(there[k]))
        def _():
            for it in range(ITERS):
                for f in range(2):
                    rcol[it, f, k - 2] = jnp.zeros((8, 128), F32)

    def make_kmat():
        i0 = lax.broadcasted_iota(jnp.int32, (segs, segs), 0)
        i1 = lax.broadcasted_iota(jnp.int32, (segs, segs), 1)

        def one(q):
            w = well_s[q]
            count = count_s[w]
            m = jnp.where(jnp.logical_and(i0 < count, i1 < count), inv[w], 0.0)
            kmat[q] = lax.dot_general(
                m,
                coef[q].astype(F32),
                (((0,), (0,)), ((), ())),
                precision=lax.Precision.HIGHEST,
                preferred_element_type=F32,
            )

        pl.loop(0, blocks, unroll=2)(one)

    def invert(f):
        def one(l):
            rdiag[f, l] = 1.0 / rdiag[f, l]

        pl.loop(0, layers)(one)

    def make_tu():
        def one(l):
            for c in range(128 // CH):
                rows = slice(c * CH, c * CH + CH)
                fl = flags[l, rows, :]
                for k in range(4):
                    bit = jnp.bitwise_and(jnp.right_shift(fl, k), 1)
                    t = trans[k, l, rows, :].astype(F32)
                    tu[k, l, rows, :] = jnp.where(bit == 1, t, 0.0).astype(BF16)

        pl.loop(0, layers)(one)

    def col_of(hrow, c):
        return jnp.concatenate(
            [lane_pick(hrow, sub8 + (c * CH + 8 * i)) for i in range(CH // 8)], axis=0
        )

    def neighbours(load, c, west_row, east_row, south_col, north_col):
        r0 = c * CH
        mid = [load(h, r0) for h in range(2)]
        if c == 0:
            west = [jnp.where(subc == 0, west_row[h], pltpu.roll(mid[h], 1, 0)) for h in range(2)]
        else:
            west = [load(h, r0 - 1) for h in range(2)]
        if c == 128 // CH - 1:
            east = [
                jnp.where(subc == CH - 1, east_row[h], pltpu.roll(mid[h], CH - 1, 0))
                for h in range(2)
            ]
        else:
            east = [load(h, r0 + 1) for h in range(2)]
        up = [pltpu.roll(x, 1, 1) for x in mid]
        down = [pltpu.roll(x, 127, 1) for x in mid]
        south = [jnp.where(lanec == 0, south_col, up[0]), jnp.where(lanec == 0, up[0], up[1])]
        north = [
            jnp.where(lanec == 127, down[1], down[0]),
            jnp.where(lanec == 127, north_col, down[1]),
        ]
        return west, east, south, north

    def p_inner(old, new):
        def one(l):
            for c in range(128 // CH):
                rows = slice(c * CH, c * CH + CH)
                near = neighbours(
                    lambda h, r: old[2 * l + h, r : r + CH, :], c, (0.0, 0.0), (0.0, 0.0), 0.0, 0.0
                )
                for h in range(2):
                    acc = p_src[2 * l + h, rows, :]
                    for k in range(4):
                        acc = acc + trans[k, l, rows, halves[h]].astype(F32) * near[k][h]
                    new[2 * l + h, rows, :] = acc * rdiag[0, l, rows, halves[h]]

        pl.loop(0, layers, unroll=2)(one)

    def halo_weights():
        for h in range(2):
            for k, r in ((W, 0), (E, 127)):
                t = trans[k, :, r - r % CH : r - r % CH + CH, halves[h]].astype(F32)
                d = rdiag[0, :, r - r % CH : r - r % CH + CH, halves[h]]
                wrows[k, h * layers : h * layers + layers] = (t * d)[:, r % CH, :]

        def one(l):
            for k, h, lane in ((S, 0, 0), (N, 1, 127)):
                acc = jnp.zeros((8, 128), F32)
                for c in range(128 // CH):
                    rows = slice(c * CH, c * CH + CH)
                    x = trans[k, l, rows, halves[h]].astype(F32) * rdiag[0, l, rows, halves[h]]
                    for i in range(CH // 8):
                        b = jnp.broadcast_to(x[8 * i : 8 * i + 8, lane : lane + 1], (8, 128))
                        acc = jnp.where(lane8 == sub8 + (c * CH + 8 * i), b, acc)
                wcols[k - 2, pl.ds(l, 1), :] = jnp.sum(acc, axis=0, keepdims=True)

        pl.loop(0, layers)(one)

    def p_rows(it, new):
        for h in range(2):
            at = slice(h * layers, h * layers + layers)
            for k, r in ((W, 0), (E, 127)):
                half_of(new, h)[:, r, :] += wrows[k, at] * rrow[it, 0, k, at]

    def p_cols(it, new):
        def one(l):
            for k, h, lane in ((S, 0, 0), (N, 1, 127)):
                at = pl.ds(l, 1)
                add = jnp.broadcast_to(wcols[k - 2, at, :] * rcol[it, 0, k - 2, at, :], (8, 128))
                for g in range(16):
                    rows = slice(8 * g, 8 * g + 8)
                    x = new[2 * l + h, rows, :]
                    new[2 * l + h, rows, :] = jnp.where(
                        lane8 == lane, x + lane_pick(add, sub8 + 8 * g), x
                    )

        pl.loop(0, layers, unroll=2)(one)

    def s_sweep(it, oldp, olds, store):
        def one(l):
            def row(k, h):
                at = pl.ds(h * layers + l, 1)
                return rrow[it, 1, k, at, :] + 0.3 * rrow[it, 0, k, at, :]

            def col(k):
                at = pl.ds(l, 1)
                x = rcol[it, 1, k - 2, at, :] + 0.3 * rcol[it, 0, k - 2, at, :]
                return jnp.broadcast_to(x, (8, 128))

            west_row = [row(W, h) for h in range(2)]
            east_row = [row(E, h) for h in range(2)]
            south, north = col(S), col(N)
            for c in range(128 // CH):
                rows = slice(c * CH, c * CH + CH)
                near = neighbours(
                    lambda h, r: olds[2 * l + h, r : r + CH, :] + 0.3 * oldp[2 * l + h, r : r + CH, :],
                    c,
                    west_row,
                    east_row,
                    col_of(south, c),
                    col_of(north, c),
                )
                for h in range(2):
                    acc = s_src[2 * l + h, rows, :]
                    p3 = 0.3 * oldp[2 * l + h, rows, :]
                    for k in range(4):
                        acc = acc + tu[k, l, rows, halves[h]].astype(F32) * (near[k][h] - p3)
                    store(l, h, rows, acc * rdiag[1, l, rows, halves[h]])

        pl.loop(0, layers, unroll=2)(one)

    def sample(new):
        flat = new.reshape(2 * layers * 128, 128)

        def one(q):
            acc = jnp.zeros((8, 128), F32)
            for g in range(16):
                blk = jnp.zeros((8, 128), F32)
                for i in range(8):
                    x = flat[pl.ds(row_idx[q, 8 * g + i], 1), :]
                    blk = jnp.where(sub8 == i, jnp.broadcast_to(x, (8, 128)), blk)
                at = lanes_r[pl.ds(pl.multiple_of(q * 128, 128) + 8 * g, 8), :]
                acc = jnp.where(lane8 == sub8 + 8 * g, lane_pick(blk, at), acc)
            samp[pl.ds(q, 1), :] = jnp.sum(acc, axis=0, keepdims=True)

        pl.loop(0, blocks, unroll=8)(one)

    def partial_sums():
        tile = jnp.zeros((8, 128), F32)
        for q in range(blocks):
            x = jnp.broadcast_to(samp[q : q + 1, :], (segs, 128)) * coef[q].astype(F32)
            for j in range(groups):
                col = jnp.sum(x[8 * j : 8 * j + 8, :], axis=1, keepdims=True)
                tile = jnp.where(lane8 == blocks * j + q, jnp.broadcast_to(col, (8, 128)), tile)
        return tile

    def corrections(it):
        for q in range(blocks):
            acc = jnp.zeros((8, 128), F32)
            for d in range(n_gy):
                acc = acc + jnp.where(wall[d] == well_s[q], ag[it, d], 0.0)
            tot = jnp.zeros((8, 128), F32)
            for j in range(groups):
                mine = jnp.where(lane8 // blocks == j, acc, 0.0)
                col = jnp.sum(mine, axis=1, keepdims=True)
                tot = tot + kmat[q, 8 * j : 8 * j + 8, :] * col
            corr[q : q + 1, :] = jnp.sum(tot, axis=0, keepdims=True)

    def spread():
        def one(i):
            at = pl.ds(pl.multiple_of(i * 32, 32), 32)
            at2 = pl.ds(pl.multiple_of(i * 32 + 256, 32), 32)
            for q in range(blocks):
                c = corr[q : q + 1, :]
                hi = c.astype(BF16)
                lo = (c - hi.astype(F32)).astype(BF16)
                v = vt[at, q * 128 : q * 128 + 128]
                cvt[at, q * 128 : q * 128 + 128] = v * hi
                cvt[at2, q * 128 : q * 128 + 128] = v * lo

        pl.loop(0, 256 // 32, unroll=2)(one)

    def dot_t(x, y):
        return lax.dot_general(x, y, (((1,), (1,)), ((), ())), preferred_element_type=F32)

    def edges_first(it):
        for q in range(blocks):
            cols = slice(q * 128, q * 128 + 128)
            c = corr[q : q + 1, :]
            hi = c.astype(BF16).astype(F32)
            lo = c - hi
            b = jnp.bitwise_and(cells[q : q + 1, :], 255)
            parts = [jnp.where(b == e, x, 0.0) for e in (0, 255) for x in (hi, lo)]
            rows = lax.broadcasted_iota(jnp.int32, (16, 128), 0)
            tile = jnp.zeros((16, 128), F32)
            for i, x in enumerate(parts):
                tile = jnp.where(rows == i, x, tile)
            edge[:, cols] = tile.astype(BF16)
        r = dot_t(edge[...], ut[...])
        for side in range(2):
            both = r[2 * side : 2 * side + 1, :] + r[2 * side + 1 : 2 * side + 2, :]
            for l in range(layers):
                scol[it, 0, side, l : l + 1, :] -= both[:, l * 128 : l * 128 + 128]
        for k in (S, N):

            @pl.when(there[k])
            def _():
                halo_copy(it, 0, k, 5 - k).start()

        spread()
        r = dot_t(ut_edge[...], cvt[...])
        for k in (W, E):
            at = slice(k * layers, k * layers + layers)
            for h in range(2):
                both = r[at, halves[h]] + r[at, 256 + h * 128 : 384 + h * 128]
                srow[it, 0, k, h * layers : h * layers + layers] -= both
        for k in (W, E):

            @pl.when(there[k])
            def _():
                halo_copy(it, 0, k, 1 - k).start()

    def scatter(new, store, done=None):
        def one(i):
            r = dot_t(ut[pl.ds(pl.multiple_of(i * MM, MM), MM), :], cvt[...])
            for j in range(MM // 128):
                l = i * (MM // 128) + j
                at = slice(j * 128, j * 128 + 128)
                for h in range(2):
                    both = r[at, halves[h]] + r[at, 256 + h * 128 : 384 + h * 128]
                    store(l, h, new[2 * l + h] - both)
            if done is not None:
                done(i)

        pl.loop(0, ut.shape[0] // MM)(one)

    def save_p(i):
        at = pl.ds(i * (MM // 128), MM // 128)
        return pltpu.make_async_copy(out_p.at[0, at], out_h.at[0, at], ld.at[1 + i])

    old_p, old_s = p_src, s_src
    spare = ((p_a, s_a), (p_b, s_b), (p_a, s_a))
    for it in range(ITERS):
        new_p, new_s = spare[it]
        if it == 0:
            load_coef.wait()
            load_inv.wait()
            make_kmat()
            load_dp.wait()
            load_t.wait()
            invert(0)
            halo_weights()
            load_ds.wait()
            load_f.wait()
            invert(1)
            make_tu()
        p_inner(old_p, new_p)
        if it == 0:
            load_rows.wait()
        halo_wait(it, 0, (W, E))
        p_rows(it, new_p)
        halo_wait(it, 0, (S, N))
        p_cols(it, new_p)
        sample(new_p)
        tile = partial_sums()
        agsend[it] = tile
        ag[it, gy] = tile
        for d in range(1, n_gy):
            peer_copy(agsend.at[it], ag.at[it, gy], ss_ag.at[it, d - 1], rs_ag.at[it, gy], d).start()
        if it == 0:
            for d in range(1, n_gy):
                peer = lax.rem(gy + d, n_gy)
                peer_copy(wsend, wall.at[peer], ss_w.at[d - 1], rs_w.at[peer], d).wait_recv()
        halo_wait(it, 1)

        def keep_s(l, h, rows, x):
            new_s[2 * l + h, rows, :] = x

        def last_s(l, h, rows, x):
            out_p[1, l, rows, halves[h]] = x

        s_sweep(it, old_p, old_s, keep_s if it < ITERS - 1 else last_s)
        if it < ITERS - 1:
            halo_pack(new_s, it + 1, 1)
            halo_start(it + 1, 1)
            halo_pack(new_p, it + 1, 0)
        else:
            save_s = pltpu.make_async_copy(out_p.at[1], out_h.at[1], ld.at[0])
            save_s.start()
        for d in range(1, n_gy):
            peer = lax.rem(gy + d, n_gy)
            peer_copy(
                agsend.at[it], ag.at[it, peer], ss_ag.at[it, d - 1], rs_ag.at[it, peer], d
            ).wait_recv()
        corrections(it)

        def keep_p(l, h, x):
            new_p[2 * l + h] = x

        def last_p(l, h, x):
            out_p[0, l, :, halves[h]] = x

        if it < ITERS - 1:
            edges_first(it + 1)
        else:
            spread()
        if it < ITERS - 1:
            scatter(new_p, keep_p)
        else:
            scatter(new_p, last_p, lambda i: save_p(i).start())
        old_p, old_s = new_p, new_s

    for d in range(1, n_gy):
        peer_copy(wsend, wall.at[gy], ss_w.at[d - 1], rs_w.at[gy], d).wait_send()
        for it in range(ITERS):
            peer_copy(
                agsend.at[it], ag.at[it, gy], ss_ag.at[it, d - 1], rs_ag.at[it, gy], d
            ).wait_send()
    for k in (W, E, S, N):

        @pl.when(there[k])
        def _():
            for it in range(ITERS):
                for f in range(2):
                    halo_copy(it, f, k, k).wait_send()

    save_s.wait()
    for i in range(ut.shape[0] // MM):
        save_p(i).wait()


def shards(
    n_gx,
    n_gy,
    source,
    transmissibility,
    diagonal,
    upwind_flags,
    panel_coef,
    perf_cell,
    panel_well,
    seg_count,
    well_inverse,
):
    layers = upwind_flags.shape[0]
    anywhere = pl.BlockSpec(memory_space=pl.ANY)
    smem = pl.BlockSpec(memory_space=pltpu.SMEM)
    dma = pltpu.SemaphoreType.DMA
    blocks, segs = panel_coef.shape[2:4]
    rows = blocks * 128
    field = pltpu.VMEM((2 * layers, 128, 128), F32)
    return pl.pallas_call(
        functools.partial(kernel, n_gx, n_gy),
        out_shape=jax.ShapeDtypeStruct(source.shape, F32),
        in_specs=[smem] * 2 + [anywhere] * 7,
        out_specs=anywhere,
        scratch_shapes=[
            field,
            field,
            field,
            field,
            field,
            field,
            pltpu.VMEM(transmissibility.shape, BF16),
            pltpu.VMEM(upwind_flags.shape, jnp.int32),
            pltpu.VMEM(diagonal.shape, F32),
            pltpu.VMEM(transmissibility.shape, BF16),
            pltpu.VMEM((blocks, segs, 128), BF16),
            pltpu.VMEM((blocks, 128), jnp.int32),
            pltpu.VMEM(well_inverse.shape[1:], F32),
            pltpu.VMEM((layers * 128, rows), BF16),
            pltpu.VMEM((256, rows), BF16),
            pltpu.VMEM((512, rows), BF16),
            pltpu.VMEM((2 * layers, rows), BF16),
            pltpu.VMEM((16, rows), BF16),
            pltpu.VMEM((2, 2 * layers, 128), F32),
            pltpu.VMEM((2, layers, 128), F32),
            pltpu.VMEM(source.shape, F32),
            pltpu.VMEM((rows, 128), jnp.int32),
            pltpu.VMEM((blocks, 128), jnp.int32),
            pltpu.SMEM((blocks, 128), jnp.int32),
            pltpu.VMEM((blocks, segs, 128), F32),
            pltpu.VMEM((blocks, 128), F32),
            pltpu.VMEM((blocks, 128), F32),
            pltpu.VMEM((ITERS, 2, 2, 2 * layers, 128), F32),
            pltpu.VMEM((ITERS, 2, 2, 2 * layers, 128), F32),
            pltpu.VMEM((ITERS, 2, 2, layers, 128), F32),
            pltpu.VMEM((ITERS, 2, 2, layers, 128), F32),
            pltpu.VMEM((8, 128), jnp.int32),
            pltpu.VMEM((n_gy, 8, 128), jnp.int32),
            pltpu.VMEM((ITERS, 8, 128), F32),
            pltpu.VMEM((ITERS, n_gy, 8, 128), F32),
            dma((12,)),
            dma((ITERS, 2, 2)),
            dma((ITERS, 2, 2)),
            dma((ITERS, 2, 2)),
            dma((ITERS, 2, 2)),
            dma((n_gy - 1,)),
            dma((n_gy,)),
            dma((ITERS, n_gy - 1)),
            dma((ITERS, n_gy)),
        ],
        compiler_params=pltpu.CompilerParams(
            collective_id=0, has_side_effects=True, vmem_limit_bytes=56 * 1024 * 1024
        ),
    )(
        panel_well[0, 0],
        seg_count[0],
        source,
        transmissibility,
        diagonal,
        upwind_flags,
        panel_coef[0, 0],
        perf_cell[0, 0],
        well_inverse[0],
    )


def solution(mesh):
    placed = (
        P(None, None, "gx", "gy"),
        P(None, None, "gx", "gy"),
        P(None, None, "gx", "gy"),
        P(None, "gx", "gy"),
        P("gx", "gy", None, None, None),
        P("gx", "gy", None, None),
        P("gx", "gy", None),
        P("gx", None),
        P("gx", None, None, None),
    )
    return jax.shard_map(
        functools.partial(shards, mesh.shape["gx"], mesh.shape["gy"]),
        mesh=mesh,
        in_specs=placed,
        out_specs=P(None, None, "gx", "gy"),
        check_vma=False,
    )
```

```python
import functools

import jax
import jax.numpy as jnp
from jax import lax
from jax.experimental import pallas as pl
from jax.experimental.pallas import tpu as pltpu
from jax.sharding import PartitionSpec as P

ITERS = 3
MESH = pl.DeviceIdType.MESH
F32 = jnp.float32
BF16 = jnp.bfloat16
W, E, S, N = 0, 1, 2, 3
CH = 16
MM = 512


def lane_pick(x, idx):
    return jnp.take_along_axis(x, idx, axis=1, mode="promise_in_bounds")


def kernel(
    n_gx,
    n_gy,
    well_s,
    count_s,
    src_h,
    trans_h,
    diag_h,
    flags_h,
    coef_h,
    cells_h,
    inv_h,
    out_h,
    p_src,
    s_src,
    p_a,
    p_b,
    s_a,
    s_b,
    trans,
    flags,
    rdiag,
    tu,
    coef,
    cells,
    inv,
    ut,
    vt,
    cvt,
    ut_edge,
    edge,
    wrows,
    wcols,
    out_p,
    lanes_r,
    row_v,
    row_idx,
    kmat,
    samp,
    corr,
    srow,
    rrow,
    scol,
    rcol,
    wsend,
    wall,
    agsend,
    ag,
    ld,
    ss_row,
    rs_row,
    ss_col,
    rs_col,
    ss_w,
    rs_w,
    ss_ag,
    rs_ag,
):
    gx = lax.axis_index("gx")
    gy = lax.axis_index("gy")
    there = (gx > 0, gx < n_gx - 1, gy > 0, gy < n_gy - 1)
    peer_id = ({"gx": gx - 1}, {"gx": gx + 1}, {"gy": gy - 1}, {"gy": gy + 1})
    layers = trans.shape[1]
    n_y = n_gy // 2
    away = [(y, 1) for y in sorted(range(n_y), key=lambda y: -min(y, n_y - y))]
    away += [(y, 0) for y in sorted(range(1, n_y), key=lambda y: -min(y, n_y - y))]
    peers = [
        lax.rem(gy // 2 + y, n_y) * 2 + lax.rem(lax.rem(gy, 2) + z, 2) for y, z in away
    ]
    blocks = coef.shape[0]
    segs = coef.shape[1]
    groups = segs // 8
    halves = (slice(0, 128), slice(128, 256))

    sub8 = lax.broadcasted_iota(jnp.int32, (8, 128), 0)
    lane8 = lax.broadcasted_iota(jnp.int32, (8, 128), 1)
    subc = lax.broadcasted_iota(jnp.int32, (CH, 128), 0)
    lanec = lax.broadcasted_iota(jnp.int32, (CH, 128), 1)

    def half_of(ref, h):
        return ref.reshape(layers, 2, 128, 128).at[:, h]

    loads = [
        pltpu.make_async_copy(src_h.at[f, :, :, halves[h]], half_of(ref, h), ld.at[2 * f + h])
        for f, ref in enumerate((p_src, s_src))
        for h in range(2)
    ]
    load_cells = pltpu.make_async_copy(cells_h, cells, ld.at[4])
    load_coef = pltpu.make_async_copy(coef_h, coef, ld.at[5])
    load_inv = pltpu.make_async_copy(inv_h, inv, ld.at[6])
    load_dp = pltpu.make_async_copy(diag_h.at[0], rdiag.at[0], ld.at[7])
    load_ds = pltpu.make_async_copy(diag_h.at[1], rdiag.at[1], ld.at[8])
    load_t = pltpu.make_async_copy(trans_h, trans, ld.at[9])
    load_f = pltpu.make_async_copy(flags_h, flags, ld.at[10])
    load_cells.start()
    for x in loads:
        x.start()
    for x in (load_coef, load_inv, load_dp, load_t, load_ds, load_f):
        x.start()

    barrier = pltpu.get_barrier_semaphore()
    for peer in peers:
        pl.semaphore_signal(barrier, inc=1, device_id={"gy": peer}, device_id_type=MESH)
    for k in (W, E):

        @pl.when(there[k])
        def _():
            pl.semaphore_signal(barrier, inc=1, device_id=peer_id[k], device_id_type=MESH)

    def halo_copy(it, f, k, dst_side):
        if k in (W, E):
            return pltpu.make_async_remote_copy(
                src_ref=srow.at[it, f, k],
                dst_ref=rrow.at[it, f, dst_side],
                send_sem=ss_row.at[it, f, k],
                recv_sem=rs_row.at[it, f, dst_side],
                device_id=peer_id[k],
                device_id_type=MESH,
            )
        return pltpu.make_async_remote_copy(
            src_ref=scol.at[it, f, k - 2],
            dst_ref=rcol.at[it, f, dst_side - 2],
            send_sem=ss_col.at[it, f, k - 2],
            recv_sem=rs_col.at[it, f, dst_side - 2],
            device_id=peer_id[k],
            device_id_type=MESH,
        )

    def halo_pack(buf, it, f):
        for h in range(2):
            for k, r in ((W, 0), (E, 127)):
                srow[it, f, k, h * layers : h * layers + layers] = half_of(buf, h)[:, r, :]

        def one(l):
            for side, half, lane in ((0, 0, 0), (1, 1, 127)):
                acc = jnp.zeros((8, 128), F32)
                for g in range(16):
                    v = buf[2 * l + half, 8 * g : 8 * g + 8, :]
                    b = jnp.broadcast_to(v[:, lane : lane + 1], (8, 128))
                    acc = jnp.where(lane8 == sub8 + 8 * g, b, acc)
                scol[it, f, side, pl.ds(l, 1), :] = jnp.sum(acc, axis=0, keepdims=True)

        pl.loop(0, layers, unroll=4)(one)

    def halo_start(it, f):
        for k in (S, N, W, E):

            @pl.when(there[k])
            def _():
                halo_copy(it, f, k, 1 - k if k < 2 else 5 - k).start()

    def halo_wait(it, f, sides=(W, E, S, N)):
        for k in sides:

            @pl.when(there[k])
            def _():
                halo_copy(it, f, k, k).wait_recv()

    def peer_copy(src_ref, dst_ref, send_sem, recv_sem, d):
        return pltpu.make_async_remote_copy(
            src_ref=src_ref,
            dst_ref=dst_ref,
            send_sem=send_sem,
            recv_sem=recv_sem,
            device_id={"gy": peers[d - 1]},
            device_id_type=MESH,
        )

    wrow = jnp.zeros((8, 128), jnp.int32)
    for q in range(blocks):
        wrow = jnp.where(lax.rem(lane8, blocks) == q, well_s[q], wrow)
    wsend[...] = wrow
    wall[gy] = wrow

    load_cells.wait()
    cell = cells[...]
    row_v[...] = (
        jnp.left_shift(jnp.right_shift(cell, 15), 8)
        + jnp.left_shift(jnp.bitwise_and(jnp.right_shift(cell, 7), 1), 7)
        + jnp.bitwise_and(jnp.right_shift(cell, 8), 127)
    )
    load_rows = pltpu.make_async_copy(row_v, row_idx, ld.at[11])
    load_rows.start()

    def lanes_of(q):
        lane = jnp.broadcast_to(jnp.bitwise_and(cells[pl.ds(q, 1), :], 127), (128, 128))
        lanes_r[pl.ds(pl.multiple_of(q * 128, 128), 128), :] = lane.T

    pl.loop(0, blocks, unroll=2)(lanes_of)

    def hot_rows(i):
        i32 = lax.broadcasted_iota(jnp.int32, (32, 128), 0) + i * 32
        for q in range(blocks):
            a = jnp.right_shift(cells[q : q + 1, :], 8)
            hot = jnp.where(i32 == a, 1.0, 0.0).astype(BF16)
            ut[pl.ds(pl.multiple_of(i * 32, 32), 32), q * 128 : q * 128 + 128] = hot

    pl.loop(0, ut.shape[0] // 32, unroll=2)(hot_rows)
    edge_row = lax.broadcasted_iota(jnp.int32, (16, 128), 0)
    edge_row = jnp.where(edge_row < layers, edge_row * 128, (edge_row - layers) * 128 + 127)
    for q in range(blocks):
        hit = edge_row == jnp.right_shift(cells[q : q + 1, :], 8)
        ut_edge[:, q * 128 : q * 128 + 128] = jnp.where(hit, 1.0, 0.0).astype(BF16)


    def hot_cols(i):
        i32 = lax.broadcasted_iota(jnp.int32, (32, 128), 0) + i * 32
        for q in range(blocks):
            b = jnp.bitwise_and(cells[q : q + 1, :], 255)
            hot = jnp.where(i32 == b, 1.0, 0.0).astype(BF16)
            vt[pl.ds(pl.multiple_of(i * 32, 32), 32), q * 128 : q * 128 + 128] = hot

    pl.loop(0, vt.shape[0] // 32, unroll=2)(hot_cols)

    for x in loads:
        x.wait()
    halo_pack(p_src, 0, 0)
    halo_pack(s_src, 0, 1)

    beside = jnp.where(there[W], 1, 0) + jnp.where(there[E], 1, 0)
    pl.semaphore_wait(barrier, n_gy - 1 + beside)
    halo_start(0, 0)
    halo_start(0, 1)
    for d in range(1, n_gy):
        peer_copy(wsend, wall.at[gy], ss_w.at[d - 1], rs_w.at[gy], d).start()

    for k in (W, E):

        @pl.when(jnp.logical_not(there[k]))
        def _():
            for it in range(ITERS):
                for f in range(2):
                    rrow[it, f, k] = jnp.zeros((16, 128), F32)

    for k in (S, N):

        @pl.when(jnp.logical_not(there[k]))
        def _():
            for it in range(ITERS):
                for f in range(2):
                    rcol[it, f, k - 2] = jnp.zeros((8, 128), F32)

    def make_kmat():
        i0 = lax.broadcasted_iota(jnp.int32, (segs, segs), 0)
        i1 = lax.broadcasted_iota(jnp.int32, (segs, segs), 1)

        def one(q):
            w = well_s[q]
            count = count_s[w]
            m = jnp.where(jnp.logical_and(i0 < count, i1 < count), inv[w], 0.0)
            kmat[q] = lax.dot_general(
                m,
                coef[q].astype(F32),
                (((0,), (0,)), ((), ())),
                precision=lax.Precision.HIGHEST,
                preferred_element_type=F32,
            )

        pl.loop(0, blocks, unroll=2)(one)

    def invert(f):
        def one(l):
            rdiag[f, l] = 1.0 / rdiag[f, l]

        pl.loop(0, layers)(one)

    def make_tu():
        def one(l):
            for c in range(128 // CH):
                rows = slice(c * CH, c * CH + CH)
                fl = flags[l, rows, :]
                for k in range(4):
                    bit = jnp.bitwise_and(jnp.right_shift(fl, k), 1)
                    t = trans[k, l, rows, :].astype(F32)
                    tu[k, l, rows, :] = jnp.where(bit == 1, t, 0.0).astype(BF16)

        pl.loop(0, layers)(one)

    def col_of(hrow, c):
        return jnp.concatenate(
            [lane_pick(hrow, sub8 + (c * CH + 8 * i)) for i in range(CH // 8)], axis=0
        )

    def neighbours(load, c, west_row, east_row, south_col, north_col):
        r0 = c * CH
        mid = [load(h, r0) for h in range(2)]
        if c == 0:
            west = [jnp.where(subc == 0, west_row[h], pltpu.roll(mid[h], 1, 0)) for h in range(2)]
        else:
            west = [load(h, r0 - 1) for h in range(2)]
        if c == 128 // CH - 1:
            east = [
                jnp.where(subc == CH - 1, east_row[h], pltpu.roll(mid[h], CH - 1, 0))
                for h in range(2)
            ]
        else:
            east = [load(h, r0 + 1) for h in range(2)]
        up = [pltpu.roll(x, 1, 1) for x in mid]
        down = [pltpu.roll(x, 127, 1) for x in mid]
        south = [jnp.where(lanec == 0, south_col, up[0]), jnp.where(lanec == 0, up[0], up[1])]
        north = [
            jnp.where(lanec == 127, down[1], down[0]),
            jnp.where(lanec == 127, north_col, down[1]),
        ]
        return west, east, south, north

    def p_inner(old, new):
        def one(l):
            for c in range(128 // CH):
                rows = slice(c * CH, c * CH + CH)
                near = neighbours(
                    lambda h, r: old[2 * l + h, r : r + CH, :], c, (0.0, 0.0), (0.0, 0.0), 0.0, 0.0
                )
                for h in range(2):
                    acc = p_src[2 * l + h, rows, :]
                    for k in range(4):
                        acc = acc + trans[k, l, rows, halves[h]].astype(F32) * near[k][h]
                    new[2 * l + h, rows, :] = acc * rdiag[0, l, rows, halves[h]]

        pl.loop(0, layers, unroll=4)(one)

    def halo_weights():
        for h in range(2):
            for k, r in ((W, 0), (E, 127)):
                t = trans[k, :, r - r % CH : r - r % CH + CH, halves[h]].astype(F32)
                d = rdiag[0, :, r - r % CH : r - r % CH + CH, halves[h]]
                wrows[k, h * layers : h * layers + layers] = (t * d)[:, r % CH, :]

        def one(l):
            for k, h, lane in ((S, 0, 0), (N, 1, 127)):
                acc = jnp.zeros((8, 128), F32)
                for c in range(128 // CH):
                    rows = slice(c * CH, c * CH + CH)
                    x = trans[k, l, rows, halves[h]].astype(F32) * rdiag[0, l, rows, halves[h]]
                    for i in range(CH // 8):
                        b = jnp.broadcast_to(x[8 * i : 8 * i + 8, lane : lane + 1], (8, 128))
                        acc = jnp.where(lane8 == sub8 + (c * CH + 8 * i), b, acc)
                wcols[k - 2, pl.ds(l, 1), :] = jnp.sum(acc, axis=0, keepdims=True)

        pl.loop(0, layers)(one)

    def p_rows(it, new):
        for h in range(2):
            at = slice(h * layers, h * layers + layers)
            for k, r in ((W, 0), (E, 127)):
                half_of(new, h)[:, r, :] += wrows[k, at] * rrow[it, 0, k, at]

    def p_cols(it, new):
        def one(l):
            for k, h, lane in ((S, 0, 0), (N, 1, 127)):
                at = pl.ds(l, 1)
                add = jnp.broadcast_to(wcols[k - 2, at, :] * rcol[it, 0, k - 2, at, :], (8, 128))
                for g in range(16):
                    rows = slice(8 * g, 8 * g + 8)
                    x = new[2 * l + h, rows, :]
                    new[2 * l + h, rows, :] = jnp.where(
                        lane8 == lane, x + lane_pick(add, sub8 + 8 * g), x
                    )

        pl.loop(0, layers, unroll=8)(one)

    def s_sweep(it, oldp, olds, store):
        def one(l):
            def row(k, h):
                at = pl.ds(h * layers + l, 1)
                return rrow[it, 1, k, at, :] + 0.3 * rrow[it, 0, k, at, :]

            def col(k):
                at = pl.ds(l, 1)
                x = rcol[it, 1, k - 2, at, :] + 0.3 * rcol[it, 0, k - 2, at, :]
                return jnp.broadcast_to(x, (8, 128))

            west_row = [row(W, h) for h in range(2)]
            east_row = [row(E, h) for h in range(2)]
            south, north = col(S), col(N)
            for c in range(128 // CH):
                rows = slice(c * CH, c * CH + CH)
                near = neighbours(
                    lambda h, r: olds[2 * l + h, r : r + CH, :] + 0.3 * oldp[2 * l + h, r : r + CH, :],
                    c,
                    west_row,
                    east_row,
                    col_of(south, c),
                    col_of(north, c),
                )
                for h in range(2):
                    acc = s_src[2 * l + h, rows, :]
                    p3 = 0.3 * oldp[2 * l + h, rows, :]
                    for k in range(4):
                        acc = acc + tu[k, l, rows, halves[h]].astype(F32) * (near[k][h] - p3)
                    store(l, h, rows, acc * rdiag[1, l, rows, halves[h]])

        pl.loop(0, layers, unroll=2)(one)

    def sample(new):
        flat = new.reshape(2 * layers * 128, 128)

        def one(q):
            acc = jnp.zeros((8, 128), F32)
            for g in range(16):
                blk = jnp.zeros((8, 128), F32)
                for i in range(8):
                    x = flat[pl.ds(row_idx[q, 8 * g + i], 1), :]
                    blk = jnp.where(sub8 == i, jnp.broadcast_to(x, (8, 128)), blk)
                at = lanes_r[pl.ds(pl.multiple_of(q * 128, 128) + 8 * g, 8), :]
                acc = jnp.where(lane8 == sub8 + 8 * g, lane_pick(blk, at), acc)
            samp[pl.ds(q, 1), :] = jnp.sum(acc, axis=0, keepdims=True)

        pl.loop(0, blocks, unroll=16)(one)

    def partial_sums():
        tile = jnp.zeros((8, 128), F32)
        for q in range(blocks):
            x = jnp.broadcast_to(samp[q : q + 1, :], (segs, 128)) * coef[q].astype(F32)
            for j in range(groups):
                col = jnp.sum(x[8 * j : 8 * j + 8, :], axis=1, keepdims=True)
                tile = jnp.where(lane8 == blocks * j + q, jnp.broadcast_to(col, (8, 128)), tile)
        return tile

    def corrections(it):
        for q in range(blocks):
            acc = jnp.zeros((8, 128), F32)
            for d in range(n_gy):
                acc = acc + jnp.where(wall[d] == well_s[q], ag[it, d], 0.0)
            tot = jnp.zeros((8, 128), F32)
            for j in range(groups):
                mine = jnp.where(lane8 // blocks == j, acc, 0.0)
                col = jnp.sum(mine, axis=1, keepdims=True)
                tot = tot + kmat[q, 8 * j : 8 * j + 8, :] * col
            corr[q : q + 1, :] = jnp.sum(tot, axis=0, keepdims=True)

    def spread():
        def one(i):
            at = pl.ds(pl.multiple_of(i * 32, 32), 32)
            at2 = pl.ds(pl.multiple_of(i * 32 + 256, 32), 32)
            for q in range(blocks):
                c = corr[q : q + 1, :]
                hi = c.astype(BF16)
                lo = (c - hi.astype(F32)).astype(BF16)
                v = vt[at, q * 128 : q * 128 + 128]
                cvt[at, q * 128 : q * 128 + 128] = v * hi
                cvt[at2, q * 128 : q * 128 + 128] = v * lo

        pl.loop(0, 256 // 32, unroll=2)(one)

    def dot_t(x, y):
        return lax.dot_general(x, y, (((1,), (1,)), ((), ())), preferred_element_type=F32)

    def edges_first(it):
        for q in range(blocks):
            cols = slice(q * 128, q * 128 + 128)
            c = corr[q : q + 1, :]
            hi = c.astype(BF16).astype(F32)
            lo = c - hi
            b = jnp.bitwise_and(cells[q : q + 1, :], 255)
            parts = [jnp.where(b == e, x, 0.0) for e in (0, 255) for x in (hi, lo)]
            rows = lax.broadcasted_iota(jnp.int32, (16, 128), 0)
            tile = jnp.zeros((16, 128), F32)
            for i, x in enumerate(parts):
                tile = jnp.where(rows == i, x, tile)
            edge[:, cols] = tile.astype(BF16)
        r = dot_t(edge[...], ut[...])
        for side in range(2):
            both = r[2 * side : 2 * side + 1, :] + r[2 * side + 1 : 2 * side + 2, :]
            for l in range(layers):
                scol[it, 0, side, l : l + 1, :] -= both[:, l * 128 : l * 128 + 128]
        for k in (S, N):

            @pl.when(there[k])
            def _():
                halo_copy(it, 0, k, 5 - k).start()

        spread()
        r = dot_t(ut_edge[...], cvt[...])
        for k in (W, E):
            at = slice(k * layers, k * layers + layers)
            for h in range(2):
                both = r[at, halves[h]] + r[at, 256 + h * 128 : 384 + h * 128]
                srow[it, 0, k, h * layers : h * layers + layers] -= both
        for k in (W, E):

            @pl.when(there[k])
            def _():
                halo_copy(it, 0, k, 1 - k).start()

    def scatter(new, store, done=None):
        def one(i):
            r = dot_t(ut[pl.ds(pl.multiple_of(i * MM, MM), MM), :], cvt[...])
            for j in range(MM // 128):
                l = i * (MM // 128) + j
                at = slice(j * 128, j * 128 + 128)
                for h in range(2):
                    both = r[at, halves[h]] + r[at, 256 + h * 128 : 384 + h * 128]
                    store(l, h, new[2 * l + h] - both)
            if done is not None:
                done(i)

        pl.loop(0, ut.shape[0] // MM)(one)

    def save_p(i):
        at = pl.ds(i * (MM // 128), MM // 128)
        return pltpu.make_async_copy(out_p.at[0, at], out_h.at[0, at], ld.at[1 + i])

    old_p, old_s = p_src, s_src
    spare = ((p_a, s_a), (p_b, s_b), (p_a, s_a))
    for it in range(ITERS):
        new_p, new_s = spare[it]
        if it == 0:
            load_coef.wait()
            load_inv.wait()
            make_kmat()
            load_dp.wait()
            load_t.wait()
            invert(0)
            halo_weights()
            load_ds.wait()
            load_f.wait()
            invert(1)
            make_tu()
        p_inner(old_p, new_p)
        if it == 0:
            load_rows.wait()
        halo_wait(it, 0, (W, E))
        p_rows(it, new_p)
        halo_wait(it, 0, (S, N))
        p_cols(it, new_p)
        sample(new_p)
        tile = partial_sums()
        agsend[it] = tile
        ag[it, gy] = tile
        for d in range(1, n_gy):
            peer_copy(agsend.at[it], ag.at[it, gy], ss_ag.at[it, d - 1], rs_ag.at[it, gy], d).start()
        if it == 0:
            for d in range(1, n_gy):
                peer = peers[d - 1]
                peer_copy(wsend, wall.at[peer], ss_w.at[d - 1], rs_w.at[peer], d).wait_recv()
        halo_wait(it, 1)

        def keep_s(l, h, rows, x):
            new_s[2 * l + h, rows, :] = x

        def last_s(l, h, rows, x):
            out_p[1, l, rows, halves[h]] = x

        s_sweep(it, old_p, old_s, keep_s if it < ITERS - 1 else last_s)
        if it < ITERS - 1:
            halo_pack(new_s, it + 1, 1)
            halo_start(it + 1, 1)
            halo_pack(new_p, it + 1, 0)
        else:
            save_s = pltpu.make_async_copy(out_p.at[1], out_h.at[1], ld.at[0])
            save_s.start()
        for d in range(1, n_gy):
            peer = peers[d - 1]
            peer_copy(
                agsend.at[it], ag.at[it, peer], ss_ag.at[it, d - 1], rs_ag.at[it, peer], d
            ).wait_recv()
        corrections(it)

        def keep_p(l, h, x):
            new_p[2 * l + h] = x

        def last_p(l, h, x):
            out_p[0, l, :, halves[h]] = x

        if it < ITERS - 1:
            edges_first(it + 1)
        else:
            spread()
        if it < ITERS - 1:
            scatter(new_p, keep_p)
        else:
            scatter(new_p, last_p, lambda i: save_p(i).start())
        old_p, old_s = new_p, new_s

    for d in range(1, n_gy):
        peer_copy(wsend, wall.at[gy], ss_w.at[d - 1], rs_w.at[gy], d).wait_send()
        for it in range(ITERS):
            peer_copy(
                agsend.at[it], ag.at[it, gy], ss_ag.at[it, d - 1], rs_ag.at[it, gy], d
            ).wait_send()
    for k in (W, E, S, N):

        @pl.when(there[k])
        def _():
            for it in range(ITERS):
                for f in range(2):
                    halo_copy(it, f, k, k).wait_send()

    save_s.wait()
    for i in range(ut.shape[0] // MM):
        save_p(i).wait()


def shards(
    n_gx,
    n_gy,
    source,
    transmissibility,
    diagonal,
    upwind_flags,
    panel_coef,
    perf_cell,
    panel_well,
    seg_count,
    well_inverse,
):
    layers = upwind_flags.shape[0]
    anywhere = pl.BlockSpec(memory_space=pl.ANY)
    smem = pl.BlockSpec(memory_space=pltpu.SMEM)
    dma = pltpu.SemaphoreType.DMA
    blocks, segs = panel_coef.shape[2:4]
    rows = blocks * 128
    field = pltpu.VMEM((2 * layers, 128, 128), F32)
    return pl.pallas_call(
        functools.partial(kernel, n_gx, n_gy),
        out_shape=jax.ShapeDtypeStruct(source.shape, F32),
        in_specs=[smem] * 2 + [anywhere] * 7,
        out_specs=anywhere,
        scratch_shapes=[
            field,
            field,
            field,
            field,
            field,
            field,
            pltpu.VMEM(transmissibility.shape, BF16),
            pltpu.VMEM(upwind_flags.shape, jnp.int32),
            pltpu.VMEM(diagonal.shape, F32),
            pltpu.VMEM(transmissibility.shape, BF16),
            pltpu.VMEM((blocks, segs, 128), BF16),
            pltpu.VMEM((blocks, 128), jnp.int32),
            pltpu.VMEM(well_inverse.shape[1:], F32),
            pltpu.VMEM((layers * 128, rows), BF16),
            pltpu.VMEM((256, rows), BF16),
            pltpu.VMEM((512, rows), BF16),
            pltpu.VMEM((2 * layers, rows), BF16),
            pltpu.VMEM((16, rows), BF16),
            pltpu.VMEM((2, 2 * layers, 128), F32),
            pltpu.VMEM((2, layers, 128), F32),
            pltpu.VMEM(source.shape, F32),
            pltpu.VMEM((rows, 128), jnp.int32),
            pltpu.VMEM((blocks, 128), jnp.int32),
            pltpu.SMEM((blocks, 128), jnp.int32),
            pltpu.VMEM((blocks, segs, 128), F32),
            pltpu.VMEM((blocks, 128), F32),
            pltpu.VMEM((blocks, 128), F32),
            pltpu.VMEM((ITERS, 2, 2, 2 * layers, 128), F32),
            pltpu.VMEM((ITERS, 2, 2, 2 * layers, 128), F32),
            pltpu.VMEM((ITERS, 2, 2, layers, 128), F32),
            pltpu.VMEM((ITERS, 2, 2, layers, 128), F32),
            pltpu.VMEM((8, 128), jnp.int32),
            pltpu.VMEM((n_gy, 8, 128), jnp.int32),
            pltpu.VMEM((ITERS, 8, 128), F32),
            pltpu.VMEM((ITERS, n_gy, 8, 128), F32),
            dma((12,)),
            dma((ITERS, 2, 2)),
            dma((ITERS, 2, 2)),
            dma((ITERS, 2, 2)),
            dma((ITERS, 2, 2)),
            dma((n_gy - 1,)),
            dma((n_gy,)),
            dma((ITERS, n_gy - 1)),
            dma((ITERS, n_gy)),
        ],
        compiler_params=pltpu.CompilerParams(
            collective_id=0, has_side_effects=True, vmem_limit_bytes=56 * 1024 * 1024
        ),
    )(
        panel_well[0, 0],
        seg_count[0],
        source,
        transmissibility,
        diagonal,
        upwind_flags,
        panel_coef[0, 0],
        perf_cell[0, 0],
        well_inverse[0],
    )


def solution(mesh):
    placed = (
        P(None, None, "gx", "gy"),
        P(None, None, "gx", "gy"),
        P(None, None, "gx", "gy"),
        P(None, "gx", "gy"),
        P("gx", "gy", None, None, None),
        P("gx", "gy", None, None),
        P("gx", "gy", None),
        P("gx", None),
        P("gx", None, None, None),
    )
    return jax.shard_map(
        functools.partial(shards, mesh.shape["gx"], mesh.shape["gy"]),
        mesh=mesh,
        in_specs=placed,
        out_specs=P(None, None, "gx", "gy"),
        check_vma=False,
    )
```
